32 devices in a mesh: azim: 8 (over z, x), frame: 4 (over y, core).
Axes of the slice: x: 2, y: 2, z: 4, core: 2. Of those that a mesh axis runs over, the one named last changes fastest.
Arguments:
- features: bfloat16 [4, 14, 112, 384], P('frame', None, 'azim'), may hold values from -6 to 6
- position_bias: float32 [169, 12], replicated, may hold values from -4 to 4
- attend_weight: bfloat16 [384, 1152], replicated, may hold values from -0.3125 to 0.3125
- output_weight: bfloat16 [384, 384], replicated, may hold values from -0.3125 to 0.3125
- merge_weight: bfloat16 [1536, 768], replicated, may hold values from -0.15625 to 0.15625
- cotangent: bfloat16 [4, 7, 56, 768], P('frame', None, 'azim'), may hold values from -6 to 6
Outputs:
- merged: bfloat16 [4, 7, 56, 768], P('frame', None, 'azim')
- feature_grad: bfloat16 [4, 14, 112, 384], P('frame', None, 'azim')
- attend_grad: float32 [442368], P(('azim', 'frame'))
- output_grad: float32 [147456], P(('azim', 'frame'))
The draws below stay inside these ranges and needn't reach their ends.
All inputs are finite; a program needn't handle non-finite values.
Results may differ from the reference program's by a relative error of at most 0.0094.
Values may be sent and summed in bfloat16 or wider, within the bound.
No kernel may reach another device: no remote copies, remote signals or barrier semaphores. Data moves between devices by JAX's collectives and lax.ppermute only.
A program may use at most 64 MiB of HBM per device.

```python
import jax
import jax.numpy as jnp
from jax import lax

C2 = 384
HEADS2 = 12
C3 = 768
ROWS = 14
COLS = 112
FRAMES = 4


def levels(own_key, dims, cuts, low, top_value):
    level = 1.0
    for dim, blocks in cuts:
        heights = jax.random.uniform(jax.random.fold_in(jax.random.fold_in(own_key, 6), dim), (blocks,), jnp.float32, low / len(cuts), top_value / len(cuts))
        level = level * jnp.repeat(jnp.exp(heights), dims[dim] // blocks).reshape((-1,) + (1,) * (len(dims) - 1 - dim))
    return level


def gaussian(rng, shape, spread, reach, shards=(), held_as=jnp.bfloat16):
    level = levels(rng, shape, shards, -0.22, 0.18) if shards else 1.0
    values = jax.random.normal(rng, shape, jnp.float32) * spread * level
    return jnp.minimum(jnp.maximum(values, -reach), reach).astype(held_as)


def setup_inputs(seed: int = 0) -> dict:
    streams_of = jax.random.split(jax.random.key(seed), 7)
    return {
        "features": gaussian(streams_of[0], (FRAMES, ROWS, COLS, C2), 1.0, 6.0, ((0, 4), (2, 8))),
        "position_bias": gaussian(streams_of[1], (169, HEADS2), 1.0, 4.0, (), jnp.float32),
        "attend_weight": gaussian(streams_of[2], (C2, 3 * C2), C2 ** -0.5, 0.3125),
        "output_weight": gaussian(streams_of[3], (C2, C2), C2 ** -0.5, 0.3125),
        "merge_weight": gaussian(streams_of[4], (4 * C2, C3), (4 * C2) ** -0.5, 0.15625),
        "cotangent": gaussian(streams_of[5], (FRAMES, ROWS // 2, COLS // 2, C3), 1.0, 6.0, ((0, 4), (2, 8))),
    }


def to_windows(grid):
    row_count, col_count, channels = grid.shape
    grid = grid.reshape(row_count // 7, 7, col_count // 7, 7, channels).transpose(0, 2, 1, 3, 4)
    return grid.reshape(row_count // 7, col_count // 7, 49, channels)

def from_windows(blocks, row_count, col_count):
    channels = blocks.shape[-1]
    grid = blocks.reshape(row_count // 7, col_count // 7, 7, 7, channels).transpose(0, 2, 1, 3, 4)
    return grid.reshape(row_count, col_count, channels)

def normalize(values):
    centred = values - lax.optimization_barrier(jnp.mean(values, -1, keepdims=True))
    inverse_std = lax.rsqrt(lax.optimization_barrier(jnp.mean(centred * centred, -1, keepdims=True)) + 1e-05)
    return (centred * inverse_std, inverse_std)

def normalize_back(normed, inverse_std, grads):
    first = lax.optimization_barrier(jnp.mean(grads, -1, keepdims=True))
    second = lax.optimization_barrier(jnp.mean(grads * normed, -1, keepdims=True))
    return inverse_std * (grads - first - normed * second)

def window_bias(position_bias, row_count):
    position = jnp.arange(49)
    pos_row = position // 7
    pos_col = position % 7
    bias_index = (pos_row[:, None] - pos_row[None, :] + 6) * 13 + (pos_col[:, None] - pos_col[None, :] + 6)
    one_hot = (bias_index.reshape(-1)[:, None] == jnp.arange(169)[None, :]).astype(position_bias.dtype)
    pos_bias = jnp.dot(one_hot, position_bias, precision=lax.Precision.HIGHEST)
    pos_bias = pos_bias.reshape(49, 49, -1).transpose(2, 0, 1)
    line_index = jnp.arange(row_count // 7)[:, None] * 7 + pos_row[None, :]
    region = (line_index >= row_count - 7).astype(jnp.int32) + (line_index >= row_count - 3).astype(jnp.int32)
    row_mask = jnp.where(region[:, :, None] == region[:, None, :], 0.0, -100.0).astype(position_bias.dtype)
    return (pos_bias, row_mask)

def merge_quads(grid):
    row_count, col_count, channels = grid.shape
    grid = grid.reshape(row_count // 2, 2, col_count // 2, 2, channels).transpose(0, 2, 3, 1, 4)
    return grid.reshape(row_count // 2, col_count // 2, 4 * channels)

def split_quads(grid, channels):
    half_rows, half_cols, _ = grid.shape
    grid = grid.reshape(half_rows, half_cols, 2, 2, channels).transpose(0, 3, 1, 2, 4)
    return grid.reshape(2 * half_rows, 2 * half_cols, channels)

def attention_forward(rolled, attend_weight, pos_bias, row_mask):
    row_count, col_count, channels = rolled.shape
    head_count = pos_bias.shape[0]
    head_size = channels // head_count
    projected = jnp.dot(rolled.reshape(-1, channels), attend_weight, preferred_element_type=jnp.float32)
    projected = projected.astype(jnp.bfloat16).reshape(row_count, col_count, 3 * channels)
    blocks = to_windows(projected)
    head_shape = blocks.shape[:3] + (head_count, head_size)
    queries = blocks[..., :channels].reshape(head_shape).astype(jnp.float32)
    key_block = blocks[..., channels:2 * channels].reshape(head_shape).astype(jnp.float32)
    value_block = blocks[..., 2 * channels:].reshape(head_shape).astype(jnp.float32)
    scores = jnp.einsum('abqhd,abkhd->abhqk', queries, key_block) * head_size ** (-0.5)
    scores = scores + pos_bias[None, None] + row_mask[:, None, None]
    probs = jax.nn.softmax(scores, -1)
    probs16 = probs.astype(jnp.bfloat16)
    attended = jnp.einsum('abhqk,abkhd->abqhd', probs16.astype(jnp.float32), value_block)
    attended = attended.astype(jnp.bfloat16).reshape(head_shape[:3] + (channels,))
    return (from_windows(attended, row_count, col_count), (queries, key_block, value_block, probs, probs16))

def attention_backward(attended_grad, saved, head_size):
    queries, key_block, value_block, probs, probs16 = saved
    row_count, col_count, channels = attended_grad.shape
    outer = to_windows(attended_grad).reshape(queries.shape).astype(jnp.float32)
    value_grad = jnp.einsum('abhqk,abqhd->abkhd', probs16.astype(jnp.float32), outer)
    score_grad = jnp.einsum('abqhd,abkhd->abhqk', outer, value_block)
    soft_grad = probs * (score_grad - lax.optimization_barrier(jnp.sum(probs * score_grad, -1, keepdims=True))) * head_size ** (-0.5)
    soft16 = soft_grad.astype(jnp.bfloat16).astype(jnp.float32)
    query_grad = jnp.einsum('abhqk,abkhd->abqhd', soft16, key_block)
    key_grad = jnp.einsum('abhqk,abqhd->abkhd', soft16, queries)
    flat_shape = queries.shape[:3] + (channels,)
    joined = jnp.concatenate([query_grad.reshape(flat_shape), key_grad.reshape(flat_shape), value_grad.reshape(flat_shape)], -1)
    return from_windows(joined.astype(jnp.bfloat16), row_count, col_count)

def token_product(left, right):
    return lax.dot_general(left.reshape(-1, left.shape[-1]), right.reshape(-1, right.shape[-1]), (((0,), (0,)), ((), ())), preferred_element_type=jnp.float32)

def frame_pass(features, cotangent, attend_weight, output_weight, merge_weight, pos_bias, row_mask):
    row_count, col_count, channels = features.shape
    head_size = channels // pos_bias.shape[0]
    normed, inverse_std = normalize(features.astype(jnp.float32))
    normed = jnp.roll(normed, (-3, -3), (0, 1))
    inverse_std = jnp.roll(inverse_std, (-3, -3), (0, 1))
    rolled = normed.astype(jnp.bfloat16)
    attended, saved = attention_forward(rolled, attend_weight, pos_bias, row_mask)
    branch = jnp.dot(attended.reshape(-1, channels), output_weight, preferred_element_type=jnp.float32)
    branch = jnp.roll(branch.reshape(row_count, col_count, channels), (3, 3), (0, 1))
    hidden = (features.astype(jnp.float32) + branch).astype(jnp.bfloat16)
    quad_normed, quad_std = normalize(merge_quads(hidden).astype(jnp.float32))
    quad16 = quad_normed.astype(jnp.bfloat16)
    out_width = merge_weight.shape[1]
    merged = jnp.dot(quad16.reshape(-1, 4 * channels), merge_weight, preferred_element_type=jnp.float32)
    merged = merged.astype(jnp.bfloat16).reshape(row_count // 2, col_count // 2, out_width)
    quad_grad_in = jnp.dot(cotangent.reshape(-1, out_width), merge_weight.T, preferred_element_type=jnp.float32)
    quad_grad = normalize_back(quad_normed, quad_std, quad_grad_in.reshape(quad_normed.shape))
    hidden_grad = split_quads(quad_grad, channels).astype(jnp.bfloat16)
    branch_grad = jnp.roll(hidden_grad, (-3, -3), (0, 1))
    output_grad = token_product(attended, branch_grad)
    attended_grad = jnp.dot(branch_grad.reshape(-1, channels), output_weight.T, preferred_element_type=jnp.float32)
    attended_grad = attended_grad.astype(jnp.bfloat16).reshape(row_count, col_count, channels)
    projected_grad = attention_backward(attended_grad, saved, head_size)
    attend_grad = token_product(rolled, projected_grad)
    normed_grad = jnp.dot(projected_grad.reshape(-1, 3 * channels), attend_weight.T, preferred_element_type=jnp.float32)
    rolled_grad = normalize_back(normed, inverse_std, normed_grad.reshape(row_count, col_count, channels))
    rolled_grad = jnp.roll(rolled_grad, (3, 3), (0, 1))
    feature_grad = (hidden_grad.astype(jnp.float32) + rolled_grad).astype(jnp.bfloat16)
    return (merged, feature_grad, attend_grad, output_grad)

def reference(features, position_bias, attend_weight, output_weight, merge_weight, cotangent):
    pos_bias, row_mask = window_bias(position_bias, ROWS)

    def one_frame(pair):
        return frame_pass(pair[0], pair[1], attend_weight, output_weight, merge_weight, pos_bias, row_mask)
    merged, feature_grad, attend_grad, output_grad = lax.map(one_frame, (features, cotangent))
    return (merged, feature_grad, lax.optimization_barrier(jnp.sum(attend_grad, 0)).reshape(-1), lax.optimization_barrier(jnp.sum(output_grad, 0)).reshape(-1))
```

```python
import jax
import jax.numpy as jnp
from jax import lax
from jax.sharding import PartitionSpec as P


def from_behind(block, axis, distance):
    devices = range(lax.axis_size(axis))
    route = [((i - distance) % len(devices), i) for i in devices]
    return lax.ppermute(block, axis, route)


def to_windows(grid):
    row_count, col_count, channels = grid.shape
    grid = grid.reshape(row_count // 7, 7, col_count // 7, 7, channels).transpose(0, 2, 1, 3, 4)
    return grid.reshape(row_count // 7, col_count // 7, 49, channels)


def from_windows(blocks, row_count, col_count):
    channels = blocks.shape[-1]
    grid = blocks.reshape(row_count // 7, col_count // 7, 7, 7, channels).transpose(0, 2, 1, 3, 4)
    return grid.reshape(row_count, col_count, channels)


def normalize(values):
    centred = values - jnp.mean(values, -1, keepdims=True)
    inverse_std = lax.rsqrt(jnp.mean(centred * centred, -1, keepdims=True) + 1e-05)
    return (centred * inverse_std, inverse_std)


def normalize_back(normed, inverse_std, grads):
    first = jnp.mean(grads, -1, keepdims=True)
    second = jnp.mean(grads * normed, -1, keepdims=True)
    return inverse_std * (grads - first - normed * second)


def window_bias(position_bias, row_count):
    position = jnp.arange(49)
    pos_row = position // 7
    pos_col = position % 7
    bias_index = (pos_row[:, None] - pos_row[None, :] + 6) * 13 + (
        pos_col[:, None] - pos_col[None, :] + 6
    )
    one_hot = (bias_index.reshape(-1)[:, None] == jnp.arange(169)[None, :]).astype(
        position_bias.dtype
    )
    pos_bias = jnp.dot(one_hot, position_bias, precision=lax.Precision.HIGHEST)
    pos_bias = pos_bias.reshape(49, 49, -1).transpose(2, 0, 1)
    line_index = jnp.arange(row_count // 7)[:, None] * 7 + pos_row[None, :]
    region = (line_index >= row_count - 7).astype(jnp.int32) + (line_index >= row_count - 3).astype(
        jnp.int32
    )
    row_mask = jnp.where(region[:, :, None] == region[:, None, :], 0.0, -100.0).astype(
        position_bias.dtype
    )
    return (pos_bias, row_mask)


def merge_quads(grid):
    row_count, col_count, channels = grid.shape
    grid = grid.reshape(row_count // 2, 2, col_count // 2, 2, channels).transpose(0, 2, 3, 1, 4)
    return grid.reshape(row_count // 2, col_count // 2, 4 * channels)


def split_quads(grid, channels):
    half_rows, half_cols, _ = grid.shape
    grid = grid.reshape(half_rows, half_cols, 2, 2, channels).transpose(0, 3, 1, 2, 4)
    return grid.reshape(2 * half_rows, 2 * half_cols, channels)


def attention_forward(rolled, attend_weight, pos_bias, row_mask):
    row_count, col_count, channels = rolled.shape
    head_count = pos_bias.shape[0]
    head_size = channels // head_count
    projected = jnp.dot(
        rolled.reshape(-1, channels), attend_weight, preferred_element_type=jnp.float32
    )
    projected = projected.astype(jnp.bfloat16).reshape(row_count, col_count, 3 * channels)
    blocks = to_windows(projected)
    head_shape = blocks.shape[:3] + (head_count, head_size)
    queries = blocks[..., :channels].reshape(head_shape)
    key_block = blocks[..., channels : 2 * channels].reshape(head_shape)
    value_block = blocks[..., 2 * channels :].reshape(head_shape)
    scores = jnp.einsum(
        "abqhd,abkhd->abhqk", queries, key_block, preferred_element_type=jnp.float32
    ) * head_size ** (-0.5)
    scores = scores + pos_bias[None, None] + row_mask[:, None, None]
    probs = jax.nn.softmax(scores, -1)
    probs16 = probs.astype(jnp.bfloat16)
    attended = jnp.einsum(
        "abhqk,abkhd->abqhd", probs16, value_block, preferred_element_type=jnp.float32
    )
    attended = attended.astype(jnp.bfloat16).reshape(head_shape[:3] + (channels,))
    return (
        from_windows(attended, row_count, col_count),
        (queries, key_block, value_block, probs, probs16),
    )


def attention_backward(attended_grad, saved, head_size):
    queries, key_block, value_block, probs, probs16 = saved
    row_count, col_count, channels = attended_grad.shape
    outer = to_windows(attended_grad).reshape(queries.shape)
    value_grad = jnp.einsum(
        "abhqk,abqhd->abkhd", probs16, outer, preferred_element_type=jnp.float32
    )
    score_grad = jnp.einsum(
        "abqhd,abkhd->abhqk", outer, value_block, preferred_element_type=jnp.float32
    )
    soft_grad = (
        probs * (score_grad - jnp.sum(probs * score_grad, -1, keepdims=True)) * head_size ** (-0.5)
    )
    soft16 = soft_grad.astype(jnp.bfloat16)
    query_grad = jnp.einsum(
        "abhqk,abkhd->abqhd", soft16, key_block, preferred_element_type=jnp.float32
    )
    key_grad = jnp.einsum("abhqk,abqhd->abkhd", soft16, queries, preferred_element_type=jnp.float32)
    flat_shape = queries.shape[:3] + (channels,)
    joined = jnp.concatenate(
        [
            query_grad.reshape(flat_shape),
            key_grad.reshape(flat_shape),
            value_grad.reshape(flat_shape),
        ],
        -1,
    )
    return from_windows(joined.astype(jnp.bfloat16), row_count, col_count)


def token_product(left, right):
    return lax.dot_general(
        left.reshape(-1, left.shape[-1]),
        right.reshape(-1, right.shape[-1]),
        (((0,), (0,)), ((), ())),
        preferred_element_type=jnp.float32,
    )


def halving_bits():
    frame_bits = lax.axis_size("frame").bit_length() - 1
    azim_bits = lax.axis_size("azim").bit_length() - 1
    bits = [("frame", bit, azim_bits + frame_bits - 1 - bit) for bit in range(frame_bits)]
    bits += [("azim", bit, azim_bits - 1 - bit) for bit in range(azim_bits)]
    order = [bits[0], bits[frame_bits]] + bits[1:frame_bits] + bits[frame_bits + 1 :][::-1]
    return order, azim_bits + frame_bits


def scatter_sum(terms):
    members = lax.axis_size(("azim", "frame"))
    widths = [term.size // members for term in terms]
    order, bit_count = halving_bits()
    joined = jnp.concatenate([term.reshape(members, -1) for term in terms], 1)
    held = joined.astype(jnp.bfloat16).reshape((2,) * bit_count + (-1,))
    for axis, bit, dim in order:
        size = lax.axis_size(axis)
        own = (lax.axis_index(axis) >> bit) & 1
        route = [(i, i ^ (1 << bit)) for i in range(size)]
        kept = lax.dynamic_slice_in_dim(held, own, 1, dim)
        sent = lax.dynamic_slice_in_dim(held, 1 - own, 1, dim)
        got = lax.ppermute(sent, axis, route)
        total = kept.astype(jnp.float32) + got.astype(jnp.float32)
        held = total.astype(jnp.bfloat16)
    total = total.reshape(-1)
    return total[: widths[0]], total[widths[0] :]


def per_device(features, position_bias, attend_weight, output_weight, merge_weight, cotangent):
    local_frame = features[0]
    row_count, col_count, channels = local_frame.shape
    head_size = channels // position_bias.shape[1]
    pos_bias, row_mask = window_bias(position_bias, row_count)
    east_cols = from_behind(local_frame[:, :3], "azim", -1)
    extended = jnp.concatenate([local_frame[:, 3:], east_cols], 1)
    normed, inverse_std = normalize(extended.astype(jnp.float32))
    normed = jnp.roll(normed, -3, 0)
    inverse_std = jnp.roll(inverse_std, -3, 0)
    rolled = normed.astype(jnp.bfloat16)
    attended, saved = attention_forward(rolled, attend_weight, pos_bias, row_mask)
    branch = jnp.dot(
        attended.reshape(-1, channels), output_weight, preferred_element_type=jnp.float32
    )
    branch = jnp.roll(branch.reshape(row_count, col_count, channels), 3, 0)
    west_part = from_behind(branch[:, col_count - 3 :].astype(jnp.bfloat16), "azim", 1).astype(
        jnp.float32
    )
    branch_own = jnp.concatenate([west_part, branch[:, : col_count - 3]], 1)
    hidden = (local_frame.astype(jnp.float32) + branch_own).astype(jnp.bfloat16)
    quad_normed, quad_std = normalize(merge_quads(hidden).astype(jnp.float32))
    quad16 = quad_normed.astype(jnp.bfloat16)
    out_width = merge_weight.shape[1]
    merged = jnp.dot(
        quad16.reshape(-1, 4 * channels), merge_weight, preferred_element_type=jnp.float32
    )
    merged = merged.astype(jnp.bfloat16).reshape(row_count // 2, col_count // 2, out_width)
    quad_grad_in = jnp.dot(
        cotangent[0].reshape(-1, out_width), merge_weight.T, preferred_element_type=jnp.float32
    )
    quad_grad = normalize_back(quad_normed, quad_std, quad_grad_in.reshape(quad_normed.shape))
    hidden_grad = split_quads(quad_grad, channels).astype(jnp.bfloat16)
    east_grads = from_behind(hidden_grad[:, :3], "azim", -1)
    branch_grad = jnp.roll(jnp.concatenate([hidden_grad[:, 3:], east_grads], 1), -3, 0)
    output_part = token_product(attended, branch_grad)
    attended_grad = jnp.dot(
        branch_grad.reshape(-1, channels), output_weight.T, preferred_element_type=jnp.float32
    )
    attended_grad = attended_grad.astype(jnp.bfloat16).reshape(row_count, col_count, channels)
    projected_grad = attention_backward(attended_grad, saved, head_size)
    attend_part = token_product(rolled, projected_grad)
    normed_grad = jnp.dot(
        projected_grad.reshape(-1, 3 * channels),
        attend_weight.T,
        preferred_element_type=jnp.float32,
    )
    rolled_grad = normalize_back(
        normed, inverse_std, normed_grad.reshape(row_count, col_count, channels)
    )
    rolled_grad = jnp.roll(rolled_grad, 3, 0)
    west_grads = from_behind(
        rolled_grad[:, col_count - 3 :].astype(jnp.bfloat16), "azim", 1
    ).astype(jnp.float32)
    rolled_own = jnp.concatenate([west_grads, rolled_grad[:, : col_count - 3]], 1)
    feature_grad = (hidden_grad.astype(jnp.float32) + rolled_own).astype(jnp.bfloat16)
    attend_grad, output_grad = scatter_sum((attend_part, output_part))
    return (merged[None], feature_grad[None], attend_grad, output_grad)


def solution(mesh):
    in_specs = (P("frame", None, "azim", None), P(), P(), P(), P(), P("frame", None, "azim", None))
    out_specs = (
        P("frame", None, "azim", None),
        P("frame", None, "azim", None),
        P(("azim", "frame")),
        P(("azim", "frame")),
    )
    return jax.shard_map(
        per_device, mesh=mesh, in_specs=in_specs, out_specs=out_specs, check_vma=False
    )
```

```python
import functools

import jax
import jax.numpy as jnp
import numpy as np
from jax import lax
from jax.experimental import pallas as pl
from jax.experimental.pallas import tpu as pltpu
from jax.sharding import PartitionSpec as P

WINDOW = 7
SHIFT = 3
SLOT = 64
LANES = 128
EPS = 1e-05


def up(value, step):
    return -(-value // step) * step


def dot(left, right):
    return lax.dot_general(left, right, (((1,), (0,)), ((), ())), preferred_element_type=jnp.float32)


def dot_t(left, right):
    return lax.dot_general(left, right, (((1,), (1,)), ((), ())), preferred_element_type=jnp.float32)


def pick(select, values):
    return dot(select, values).astype(jnp.bfloat16)


class Grid:
    def __init__(self, rows, cols, heads, channels):
        self.rows, self.cols, self.heads, self.channels = rows, cols, heads, channels
        self.bands = rows // WINDOW
        self.own_across = cols // WINDOW
        self.east, self.west = 2 * WINDOW - SHIFT - 1, WINDOW - SHIFT
        own = [(a, w) for a in range(self.bands) for w in range(1, self.own_across + 1)]
        halo = [(a, w) for w in (0, self.own_across + 1) for a in range(self.bands)]
        self.windows = own + halo
        self.own_windows = len(own)
        self.stride = up(cols, 16)
        self.own_rows = rows * self.stride
        self.east_rows = up(rows * self.east, 16)
        self.west_rows = up(rows * self.west, 16)
        self.token_rows = self.own_rows + self.east_rows + self.west_rows
        self.quad_rows, self.quad_cols = rows // 2, cols // 2
        self.quad_stride = up(self.quad_cols + 1, 8)
        self.quad_count = up(self.quad_rows * (self.quad_stride + 1), 16)
        self.cot_stride = up(self.quad_cols, 16)
        self.cot_own = self.quad_rows * self.cot_stride
        self.cot_halo = up(2 * self.quad_rows, 16)
        self.back_rows = up(rows * SHIFT, 16)

    def source(self, row, col):
        if col < 0:
            return self.own_rows + self.east_rows + row * self.west + col + self.west
        if col < self.cols:
            return row * self.stride + col
        return self.own_rows + row * self.east + col - self.cols

    def window_row(self, row, col):
        line = (row - SHIFT) % self.rows
        across, place = divmod(col + self.west, WINDOW)
        window = self.windows.index((line // WINDOW, across))
        return window * SLOT + (line % WINDOW) * WINDOW + place

    def quad_row(self, row, col):
        i, j = row // 2, col // 2
        phase = 2 * (col % 2) + row % 2
        at = i * self.quad_stride + j if j < self.quad_stride else self.quad_rows * self.quad_stride + i
        return phase * self.quad_count + at

    def onehot(self, shape, pairs):
        out = np.zeros(shape, np.float32)
        for i, j in pairs:
            out[i, j] = 1
        return jnp.asarray(out, jnp.bfloat16)

    def cells(self, first, last):
        return [(r, c) for r in range(self.rows) for c in range(first, last)]

    def to_windows(self):
        cells = self.cells(-self.west, self.cols + self.east)
        pairs = [(self.window_row(r, c), self.source(r, c)) for r, c in cells]
        return self.onehot((len(self.windows) * SLOT, self.token_rows), pairs)

    def to_quads(self):
        cells = self.cells(0, self.cols + 4)
        pairs = [(self.quad_row(r, c), self.window_row(r, c)) for r, c in cells]
        return self.onehot((4 * self.quad_count, len(self.windows) * SLOT), pairs)

    def from_quads(self):
        cells = self.cells(SHIFT, self.cols + SHIFT)
        pairs = [(self.window_row(r, c), self.quad_row(r, c)) for r, c in cells]
        return self.onehot((self.own_windows * SLOT, 4 * self.quad_count), pairs)

    def quads_to_grid(self):
        pairs = [(self.source(r, c), self.quad_row(r, c)) for r, c in self.cells(0, self.cols)]
        return self.onehot((self.own_rows, 4 * self.quad_count), pairs)

    def windows_to_grid(self):
        pairs = [(self.source(r, c), self.window_row(r, c)) for r, c in self.cells(SHIFT, self.cols)]
        return self.onehot((self.own_rows, self.own_windows * SLOT), pairs)

    def windows_to_back(self):
        cells = self.cells(self.cols, self.cols + SHIFT)
        pairs = [(r * SHIFT + c - self.cols, self.window_row(r, c)) for r, c in cells]
        return self.onehot((self.back_rows, self.own_windows * SLOT), pairs)

    def back_to_grid(self):
        pairs = [(self.source(r, c), r * SHIFT + c) for r, c in self.cells(0, SHIFT)]
        return self.onehot((self.own_rows, self.back_rows), pairs)

    def pack_east(self):
        pairs = [(r * self.east + c, self.source(r, c)) for r, c in self.cells(0, self.east)]
        return self.onehot((self.east_rows, self.own_rows), pairs)

    def pack_west(self):
        first = self.cols - self.west
        pairs = [(r * self.west + c - first, self.source(r, c)) for r, c in self.cells(first, self.cols)]
        return self.onehot((self.west_rows, self.own_rows), pairs)

    def pack_cot(self):
        pairs = [(2 * i + j, i * self.cot_stride + j) for i in range(self.quad_rows) for j in range(2)]
        return self.onehot((self.cot_halo, self.cot_own), pairs)

    def cot_to_quads(self):
        pairs = []
        for i in range(self.quad_rows):
            for j in range(self.quad_cols + 2):
                own = i * self.cot_stride + j
                source = own if j < self.quad_cols else self.cot_own + 2 * i + j - self.quad_cols
                pairs.append((self.quad_row(2 * i, 2 * j), source))
        return self.onehot((self.quad_count, self.cot_own + self.cot_halo), pairs)


def normalize(values):
    centred = values - jnp.mean(values, -1, keepdims=True)
    inverse_std = lax.rsqrt(jnp.mean(centred * centred, -1, keepdims=True) + EPS)
    return centred * inverse_std, inverse_std


def spread(ref, grid_ref, stride):
    ref[0 : grid_ref.shape[0] * stride, :] = jnp.zeros((grid_ref.shape[0] * stride, ref.shape[1]), ref.dtype)
    for line in range(grid_ref.shape[0]):
        ref[line * stride : line * stride + grid_ref.shape[1], :] = grid_ref[line]


def pre_kernel(grid, x, cot, pack_east, pack_west, pack_cot, to_prev, to_next, tokens, quads):
    spread(tokens, x, grid.stride)
    spread(quads, cot, grid.cot_stride)
    channels = grid.channels
    to_prev[0 : grid.east_rows, :] = pick(pack_east[...], tokens[...])
    halo = pick(pack_cot[...], quads[...])
    for part in range(halo.shape[1] // channels):
        first = grid.east_rows + part * grid.cot_halo
        to_prev[first : first + grid.cot_halo, :] = halo[:, part * channels : (part + 1) * channels]
    to_next[...] = pick(pack_west[...], tokens[...])


def head_sum(stacked, head_mask, per_group):
    total = None
    for head in range(per_group):
        part = stacked[head * SLOT : (head + 1) * SLOT, :]
        part = jnp.where(head_mask[head * SLOT : (head + 1) * SLOT, :] > 0, part, 0.0)
        total = part if total is None else total + part
    return total


def main_kernel(
    grid, x, from_east, from_west, cot, attend_weight, output_weight, merge_weight, bias, mask, head_mask,
    to_windows, to_quads, from_quads, cot_to_quads, row_order,
    kept, sent, projected_grad, normed_out, std_out, hidden_grad_out, quad16_out,
    tokens, quads, projected, attended, probs, outer,
):
    channels, heads = grid.channels, grid.heads
    head_size = channels // heads
    scale = head_size ** (-0.5)
    per_group = LANES // head_size
    groups = heads // per_group
    own = grid.own_windows * SLOT
    total_windows = len(grid.windows)

    spread(tokens, x, grid.stride)
    tokens[grid.own_rows : grid.own_rows + grid.east_rows, :] = from_east[0 : grid.east_rows, :]
    tokens[grid.own_rows + grid.east_rows :, :] = from_west[...]
    spread(quads, cot, grid.cot_stride)
    for part in range(cot.shape[2] // channels):
        first = grid.east_rows + part * grid.cot_halo
        quads[grid.cot_own :, part * channels : (part + 1) * channels] = from_east[first : first + grid.cot_halo, :]

    windowed = dot(to_windows[...], tokens[...])
    normed, inverse_std = normalize(windowed)
    rolled = normed.astype(jnp.bfloat16)
    normed_out[...] = normed[:own]
    std_out[...] = inverse_std[:own]
    projected[...] = dot(rolled, attend_weight[...]).astype(jnp.bfloat16)

    mask_all = head_mask[...]

    def forward(window, carry):
        rows = pl.ds(pl.multiple_of(window * SLOT, SLOT), SLOT)
        band = jnp.where(
            window < grid.own_windows, window // grid.own_across, (window - grid.own_windows) % grid.bands
        )
        extra = mask[band]
        for group in range(groups):
            lanes = group * LANES
            query = projected[rows, lanes : lanes + LANES]
            key = projected[rows, channels + lanes : channels + lanes + LANES]
            value = projected[rows, 2 * channels + lanes : 2 * channels + lanes + LANES]
            spread_query = jnp.concatenate([query] * per_group, 0) * mask_all
            scores = dot_t(key, spread_query) * scale + bias[group] + extra
            weights = jnp.exp(scores - jnp.max(scores, 0, keepdims=True))
            prob = weights / jnp.sum(weights, 0, keepdims=True)

            @pl.when(window < grid.own_windows)
            def _():
                probs[jnp.minimum(window, grid.own_windows - 1) * groups + group] = prob

            mixed = dot(prob.astype(jnp.bfloat16).T, value)
            attended[rows, lanes : lanes + LANES] = head_sum(mixed, mask_all, per_group).astype(jnp.bfloat16)
        return carry

    lax.fori_loop(0, total_windows, forward, 0)

    attended_quads = pick(to_quads[...], attended[...])
    feature_quads = dot(to_quads[...], windowed.astype(jnp.bfloat16))
    branch = dot(attended_quads, output_weight[...])
    hidden = (feature_quads + branch).astype(jnp.bfloat16).astype(jnp.float32)
    count = grid.quad_count
    phases = [hidden[k * count : (k + 1) * count] for k in range(4)]
    width = 4 * channels
    mean = sum(jnp.sum(phase, -1, keepdims=True) for phase in phases) / width
    centred = [phase - mean for phase in phases]
    variance = sum(jnp.sum(phase * phase, -1, keepdims=True) for phase in centred) / width
    quad_std = lax.rsqrt(variance + EPS)
    quad_normed = [phase * quad_std for phase in centred]
    cot_quads = pick(cot_to_quads[...], quads[...])
    quad_grads = []
    for k in range(4):
        quad16_out[k * count : (k + 1) * count, :] = quad_normed[k].astype(jnp.bfloat16)
        quad_grads.append(dot_t(cot_quads, merge_weight[k * channels : (k + 1) * channels, :]))
    first = sum(jnp.sum(part, -1, keepdims=True) for part in quad_grads) / width
    second = sum(jnp.sum(part * n, -1, keepdims=True) for part, n in zip(quad_grads, quad_normed)) / width
    for k in range(4):
        hidden_grad_out[k * count : (k + 1) * count, :] = (
            quad_std * (quad_grads[k] - first - quad_normed[k] * second)
        ).astype(jnp.bfloat16)

    branch_grad = pick(from_quads[...], hidden_grad_out[...])
    outer[...] = dot_t(branch_grad, output_weight[...]).astype(jnp.bfloat16)

    def backward(window, carry):
        rows = pl.ds(pl.multiple_of(window * SLOT, SLOT), SLOT)
        for group in range(groups):
            lanes = group * LANES
            query = projected[rows, lanes : lanes + LANES]
            key = projected[rows, channels + lanes : channels + lanes + LANES]
            value = projected[rows, 2 * channels + lanes : 2 * channels + lanes + LANES]
            grads = outer[rows, lanes : lanes + LANES]
            spread_query = jnp.concatenate([query] * per_group, 0) * mask_all
            spread_grads = jnp.concatenate([grads] * per_group, 0) * mask_all
            prob = probs[window * groups + group]
            value_grad = dot(prob.astype(jnp.bfloat16), spread_grads)
            score_grad = dot_t(value, spread_grads)
            inner = jnp.sum(prob * score_grad, 0, keepdims=True)
            soft = (prob * (score_grad - inner) * scale).astype(jnp.bfloat16)
            key_grad = dot(soft, spread_query)
            query_grad = head_sum(dot(soft.T, key), mask_all, per_group)
            projected_grad[rows, lanes : lanes + LANES] = query_grad.astype(jnp.bfloat16)
            projected_grad[rows, channels + lanes : channels + lanes + LANES] = key_grad.astype(jnp.bfloat16)
            projected_grad[rows, 2 * channels + lanes : 2 * channels + lanes + LANES] = value_grad.astype(
                jnp.bfloat16
            )
        return carry

    lax.fori_loop(0, grid.own_windows, backward, 0)

    columns = lax.broadcasted_iota(jnp.int32, (channels, channels), 1)
    order = jnp.where(columns == row_order[...], 1.0, 0.0).astype(jnp.bfloat16)
    rolled_t = dot_t(order, rolled[:own]).astype(jnp.bfloat16)
    attended_t = dot_t(order, attended[0:own, :]).astype(jnp.bfloat16)
    attend_part = dot(rolled_t, projected_grad[...]).astype(jnp.bfloat16)
    output_part = dot(attended_t, branch_grad).astype(jnp.bfloat16)
    half = channels // 2
    kept[:, 0 : 3 * channels] = attend_part[:half]
    sent[:, 0 : 3 * channels] = attend_part[half:]
    kept[:, 3 * channels :] = output_part[:half]
    sent[:, 3 * channels :] = output_part[half:]


def tail_kernel(
    grid, projected_grad, attend_weight, normed, inverse_std, hidden_grad, quad16, merge_weight,
    quads_to_grid, windows_to_grid, windows_to_back, part, back, merged,
):
    channels = grid.channels
    grads = dot_t(projected_grad[...], attend_weight[...])
    n = normed[...]
    first = jnp.mean(grads, -1, keepdims=True)
    second = jnp.mean(grads * n, -1, keepdims=True)
    rolled_grad = inverse_std[...] * (grads - first - n * second)
    high = rolled_grad.astype(jnp.bfloat16)
    low = (rolled_grad - high.astype(jnp.float32)).astype(jnp.bfloat16)
    back[...] = pick(windows_to_back[...], high)
    part[...] = (
        dot(quads_to_grid[...], hidden_grad[...])
        + dot(windows_to_grid[...], high)
        + dot(windows_to_grid[...], low)
    )
    count = grid.quad_count
    total = None
    for k in range(4):
        term = dot(quad16[k * count : (k + 1) * count, :], merge_weight[k * channels : (k + 1) * channels, :])
        total = term if total is None else total + term
    for i in range(grid.quad_rows):
        first_row = i * grid.quad_stride
        merged[i] = total[first_row : first_row + grid.quad_cols].astype(jnp.bfloat16)


def last_kernel(grid, part, back, back_to_grid, out):
    total = part[...] + dot(back_to_grid[...], back[...])
    for line in range(grid.rows):
        out[line] = total[line * grid.stride : line * grid.stride + grid.cols].astype(jnp.bfloat16)


def call(kernel, outs, *args, scratch=()):
    whole = pl.BlockSpec(memory_space=pltpu.VMEM)
    return pl.pallas_call(
        kernel,
        out_shape=outs,
        in_specs=[whole] * len(args),
        out_specs=jax.tree.map(lambda _: whole, outs),
        scratch_shapes=scratch,
        compiler_params=pltpu.CompilerParams(vmem_limit_bytes=56 * 2**20),
    )(*args)


def f32(*shape):
    return jax.ShapeDtypeStruct(shape, jnp.float32)


def b16(*shape):
    return jax.ShapeDtypeStruct(shape, jnp.bfloat16)


def window_bias(position_bias, grid):
    tokens = WINDOW * WINDOW
    place = np.arange(SLOT)
    row, col = place // WINDOW, place % WINDOW
    span = 2 * WINDOW - 1
    index = (row[None, :] - row[:, None] + WINDOW - 1) * span + (col[None, :] - col[:, None] + WINDOW - 1)
    real = (place[:, None] < tokens) & (place[None, :] < tokens)
    index = np.where(real, index, 0)
    one_hot = jnp.asarray(index.reshape(-1)[:, None] == np.arange(span * span)[None, :]).astype(jnp.float32)
    heads = grid.heads
    values = jnp.dot(one_hot, position_bias, precision=lax.Precision.HIGHEST)
    per_group = LANES // (grid.channels // heads)
    values = values.reshape(SLOT, SLOT, heads // per_group, per_group).transpose(2, 0, 3, 1)
    values = values.reshape(heads // per_group, SLOT, per_group * SLOT)
    padded = jnp.asarray(np.where(place < tokens, 0.0, -1e30), jnp.float32)
    values = values + padded[None, :, None]
    line = np.arange(grid.bands)[:, None] * WINDOW + row[None, :]
    region = (line >= grid.rows - WINDOW).astype(int) + (line >= grid.rows - SHIFT).astype(int)
    blocked = np.where(region[:, :, None] == region[:, None, :], 0.0, -100.0)
    blocked = np.where(real[None], blocked, 0.0)
    mask = jnp.asarray(np.concatenate([blocked] * per_group, 2), jnp.float32)
    return values, mask


def halving_bits():
    frame_bits = lax.axis_size("frame").bit_length() - 1
    azim_bits = lax.axis_size("azim").bit_length() - 1
    frame = [("frame", bit, 1 << bit) for bit in range(frame_bits)]
    azim = [("azim", bit, 1 << (bit + frame_bits)) for bit in range(azim_bits)]
    return frame[:1] + azim[:1] + frame[1:] + azim[1:][::-1]


def row_order(channels):
    bits = halving_bits()
    members = 1 << len(bits)
    row = np.arange(channels)
    if channels % members:
        return jnp.asarray(row, jnp.int32)[:, None]
    each = channels // members
    piece = jnp.zeros(channels, jnp.int32)
    for stage, (axis, bit, weight) in enumerate(bits):
        far = (row // each >> (len(bits) - 1 - stage)) & 1
        own = (lax.axis_index(axis) >> bit) & 1
        piece = piece + (own ^ jnp.asarray(far, jnp.int32)) * weight
    return (piece * each + jnp.asarray(row % each, jnp.int32))[:, None]


def scatter_flat(terms):
    bits = halving_bits()
    members = 1 << len(bits)
    widths = [term.size // members for term in terms]
    held = jnp.concatenate([term.reshape(members, -1) for term in terms], 1)
    held = held.reshape((2,) * len(bits) + (-1,))
    for axis, bit, weight in bits:
        dim = len(bits) - weight.bit_length()
        own = (lax.axis_index(axis) >> bit) & 1
        kept = lax.dynamic_slice_in_dim(held, own, 1, dim)
        sent = lax.dynamic_slice_in_dim(held, 1 - own, 1, dim)
        got = lax.ppermute(sent, axis, [(i, i ^ (1 << bit)) for i in range(lax.axis_size(axis))])
        total = kept.astype(jnp.float32) + got.astype(jnp.float32)
        held = total.astype(jnp.bfloat16)
    total = total.reshape(-1)
    return total[: widths[0]], total[widths[0] :]


def scatter_sum(kept, sent, channels):
    if channels % (1 << len(halving_bits())):
        whole = jnp.concatenate([kept, sent], 0)
        return scatter_flat((whole[:, : 3 * channels], whole[:, 3 * channels :]))
    for axis, bit, _ in halving_bits():
        route = [(i, i ^ (1 << bit)) for i in range(lax.axis_size(axis))]
        got = lax.ppermute(sent, axis, route)
        total = kept.astype(jnp.float32) + got.astype(jnp.float32)
        half = total.shape[0] // 2
        held = total.astype(jnp.bfloat16)
        kept, sent = held[:half], held[half:]
    return total[:, : 3 * channels].reshape(-1), total[:, 3 * channels :].reshape(-1)


def from_behind(block, axis, distance):
    size = lax.axis_size(axis)
    return lax.ppermute(block, axis, [((i - distance) % size, i) for i in range(size)])


def per_device(features, position_bias, attend_weight, output_weight, merge_weight, cotangent):
    x, cot = features[0], cotangent[0]
    rows, cols, channels = x.shape
    heads = position_bias.shape[1]
    grid = Grid(rows, cols, heads, channels)
    width = cot.shape[2]
    bf16 = jnp.bfloat16
    halo_rows = grid.east_rows + width // channels * grid.cot_halo
    to_prev, to_next = call(
        functools.partial(pre_kernel, grid),
        (b16(halo_rows, channels), b16(grid.west_rows, channels)),
        x, cot, grid.pack_east(), grid.pack_west(), grid.pack_cot(),
        scratch=[pltpu.VMEM((grid.own_rows, channels), bf16), pltpu.VMEM((grid.cot_own, width), bf16)],
    )
    from_east = from_behind(to_prev, "azim", -1)
    from_west = from_behind(to_next, "azim", 1)
    bias, mask = window_bias(position_bias, grid)
    per_group = LANES * heads // channels
    lane_head = np.arange(LANES) // (channels // heads)
    head_mask = jnp.asarray(np.repeat(np.arange(per_group), SLOT)[:, None] == lane_head[None, :]).astype(bf16)
    own = grid.own_windows * SLOT
    everything = len(grid.windows) * SLOT
    quad_rows = 4 * grid.quad_count
    half = channels // 2
    kept, sent, projected_grad, normed, inverse_std, hidden_grad, quad16 = call(
        functools.partial(main_kernel, grid),
        (
            b16(half, 4 * channels), b16(half, 4 * channels), b16(own, 3 * channels), f32(own, channels),
            f32(own, 1), b16(quad_rows, channels), b16(quad_rows, channels),
        ),
        x, from_east, from_west, cot, attend_weight, output_weight, merge_weight, bias, mask, head_mask,
        grid.to_windows(), grid.to_quads(), grid.from_quads(), grid.cot_to_quads(), row_order(channels),
        scratch=[
            pltpu.VMEM((grid.token_rows, channels), bf16),
            pltpu.VMEM((grid.cot_own + grid.cot_halo, width), bf16),
            pltpu.VMEM((everything, 3 * channels), bf16),
            pltpu.VMEM((everything, channels), bf16),
            pltpu.VMEM((grid.own_windows * heads // per_group, SLOT, per_group * SLOT), jnp.float32),
            pltpu.VMEM((own, channels), bf16),
        ],
    )
    part, back, merged = call(
        functools.partial(tail_kernel, grid),
        (f32(grid.own_rows, channels), b16(grid.back_rows, channels), b16(grid.quad_rows, grid.quad_cols, width)),
        projected_grad, attend_weight, normed, inverse_std, hidden_grad, quad16, merge_weight,
        grid.quads_to_grid(), grid.windows_to_grid(), grid.windows_to_back(),
    )
    came_back = from_behind(back, "azim", 1)
    feature_grad = call(
        functools.partial(last_kernel, grid), b16(rows, cols, channels), part, came_back, grid.back_to_grid()
    )
    attend_grad, output_grad = scatter_sum(kept, sent, channels)
    return (merged[None], feature_grad[None], attend_grad, output_grad)


def solution(mesh):
    in_specs = (P("frame", None, "azim", None), P(), P(), P(), P(), P("frame", None, "azim", None))
    out_specs = (
        P("frame", None, "azim", None),
        P("frame", None, "azim", None),
        P(("azim", "frame")),
        P(("azim", "frame")),
    )
    return jax.shard_map(
        per_device, mesh=mesh, in_specs=in_specs, out_specs=out_specs, check_vma=False
    )
```

```python
import functools

import jax
import jax.numpy as jnp
import numpy as np
from jax import lax
from jax.experimental import pallas as pl
from jax.experimental.pallas import tpu as pltpu
from jax.sharding import PartitionSpec as P

WINDOW = 7
SHIFT = 3
SLOT = 64
LANES = 128
EPS = 1e-05


def up(value, step):
    return -(-value // step) * step


def dot(left, right):
    return lax.dot_general(left, right, (((1,), (0,)), ((), ())), preferred_element_type=jnp.float32)


def dot_t(left, right):
    return lax.dot_general(left, right, (((1,), (1,)), ((), ())), preferred_element_type=jnp.float32)


def pick(select, values):
    return dot(select, values).astype(jnp.bfloat16)


class Grid:
    def __init__(self, rows, cols, heads, channels):
        self.rows, self.cols, self.heads, self.channels = rows, cols, heads, channels
        self.west = WINDOW - SHIFT
        self.last = cols - self.west
        self.bands, self.across = rows // WINDOW, cols // WINDOW
        self.windows = self.bands * self.across
        self.window_rows = self.windows * SLOT
        self.stride = up(cols, 16)
        self.own_rows = rows * self.stride
        self.west_rows = up(rows * self.west, 16)
        self.quad_lines, self.quad_cols, self.quad_west = rows // 2, cols // 2, self.west // 2
        self.quad_stride = up(self.quad_cols, 8)
        self.quad_count = up(self.quad_lines * self.quad_stride, 16)
        self.cot_stride = up(self.quad_cols, 16)
        self.cot_own = self.quad_lines * self.cot_stride
        self.cot_halo = up(self.quad_west * self.quad_lines, 16)

    def source(self, row, col):
        return row * self.stride + col if col >= 0 else self.own_rows + row * self.west + col + self.west

    def window_row(self, row, col):
        line = (row - SHIFT) % self.rows
        across, place = divmod(col + self.west, WINDOW)
        window = line // WINDOW * self.across + across
        return window * SLOT + line % WINDOW * (WINDOW + 1) + place

    def quad_row(self, row, col):
        phase = 2 * (col % 2) + row % 2
        return phase * self.quad_count + row // 2 * self.quad_stride + (col + self.west) // 2

    def onehot(self, shape, pairs):
        out = np.zeros(shape, np.float32)
        for i, j in pairs:
            out[i, j] = 1
        return jnp.asarray(out, jnp.bfloat16)

    def cells(self, first, last):
        return [(r, c) for r in range(self.rows) for c in range(first, last)]

    def to_windows(self):
        pairs = [(self.window_row(r, c), self.source(r, c)) for r, c in self.cells(-self.west, self.last)]
        return self.onehot((self.window_rows, self.own_rows + self.west_rows), pairs)

    def to_quads(self):
        pairs = [(self.quad_row(r, c), self.window_row(r, c)) for r, c in self.cells(-self.west, self.last)]
        return self.onehot((4 * self.quad_count, self.window_rows), pairs)

    def from_quads(self):
        return self.to_quads().T

    def pack_tokens(self):
        pairs = [
            (r * self.west + c - self.last, self.source(r, c)) for r, c in self.cells(self.last, self.cols)
        ]
        return self.onehot((self.west_rows, self.own_rows), pairs)

    def quad_cells(self, first, last):
        return [(i, j) for i in range(self.quad_lines) for j in range(first, last)]

    def pack_cot(self):
        first = self.quad_cols - self.quad_west
        pairs = [
            (self.quad_west * i + j - first, i * self.cot_stride + j)
            for i, j in self.quad_cells(first, self.quad_cols)
        ]
        return self.onehot((self.cot_halo, self.cot_own), pairs)

    def cot_to_quads(self):
        pairs = [
            (i * self.quad_stride + j, self.cot_own + self.quad_west * i + j)
            for i, j in self.quad_cells(0, self.quad_west)
        ]
        pairs += [
            (i * self.quad_stride + j, i * self.cot_stride + j - self.quad_west)
            for i, j in self.quad_cells(self.quad_west, self.quad_cols)
        ]
        return self.onehot((self.quad_count, self.cot_own + self.cot_halo), pairs)

    def tokens_back(self):
        pairs = [(r * self.west + c + self.west, self.window_row(r, c)) for r, c in self.cells(-self.west, 0)]
        return self.onehot((self.west_rows, self.window_rows), pairs)

    def quads_back(self):
        pairs = [
            (self.quad_west * i + j, i * self.quad_stride + j) for i, j in self.quad_cells(0, self.quad_west)
        ]
        return self.onehot((self.cot_halo, self.quad_count), pairs)

    def final_tokens(self):
        pairs = [(self.source(r, c), self.window_row(r, c)) for r, c in self.cells(0, self.last)]
        pairs += [
            (self.source(r, c), self.window_rows + r * self.west + c - self.last)
            for r, c in self.cells(self.last, self.cols)
        ]
        return self.onehot((self.own_rows, self.window_rows + self.west_rows), pairs)

    def final_quads(self):
        first = self.quad_cols - self.quad_west
        pairs = [
            (i * self.quad_stride + j, i * self.quad_stride + j + self.quad_west)
            for i, j in self.quad_cells(0, first)
        ]
        pairs += [
            (i * self.quad_stride + j, self.quad_count + self.quad_west * i + j - first)
            for i, j in self.quad_cells(first, self.quad_cols)
        ]
        return self.onehot((self.quad_count, self.quad_count + self.cot_halo), pairs)


def normalize(values):
    centred = values - jnp.mean(values, -1, keepdims=True)
    inverse_std = lax.rsqrt(jnp.mean(centred * centred, -1, keepdims=True) + EPS)
    return centred * inverse_std, inverse_std


def spread(ref, grid_ref, stride):
    ref[0 : grid_ref.shape[0] * stride, :] = jnp.zeros((grid_ref.shape[0] * stride, ref.shape[1]), ref.dtype)
    for line in range(grid_ref.shape[0]):
        ref[line * stride : line * stride + grid_ref.shape[1], :] = grid_ref[line]


def pack(grid, out, tokens, quads):
    out[0 : grid.west_rows, :] = tokens
    for part in range(quads.shape[1] // grid.channels):
        first = grid.west_rows + part * grid.cot_halo
        out[first : first + grid.cot_halo, :] = quads[:, part * grid.channels : (part + 1) * grid.channels]


def unpack(grid, ref, width):
    first = grid.west_rows
    parts = [
        ref[first + part * grid.cot_halo : first + (part + 1) * grid.cot_halo, :]
        for part in range(width // grid.channels)
    ]
    return ref[0 : grid.west_rows, :], jnp.concatenate(parts, 1)


def pre_kernel(grid, x, cot, pack_tokens, pack_cot, to_next, tokens, quads):
    spread(tokens, x.get(), grid.stride)
    spread(quads, cot.get(), grid.cot_stride)
    halo = pick(pack_cot.get()[...], quads[...])
    pack(grid, to_next.ref, pick(pack_tokens.get()[...], tokens[...]), halo)
    to_next.send()


def head_sum(stacked, head_mask, per_group):
    total = None
    for head in range(per_group):
        part = stacked[head * SLOT : (head + 1) * SLOT, :]
        part = jnp.where(head_mask[head * SLOT : (head + 1) * SLOT, :] > 0, part, 0.0)
        total = part if total is None else total + part
    return total


def main_kernel(
    grid, x, from_west, to_windows, attend_weight, head_mask, bias, mask, to_quads, output_weight, cot,
    cot_to_quads, merge_weight, from_quads, order_a, order_b,
    kept, sent, projected_grad_out, normed_out, std_out, branch_grad_out, quad16_out,
    tokens, quads, projected, attended, probs, outer,
):
    channels, heads = grid.channels, grid.heads
    head_size = channels // heads
    scale = head_size ** (-0.5)
    per_group = LANES // head_size
    groups = heads // per_group

    spread(tokens, x.get(), grid.stride)
    west_tokens, west_quads = unpack(grid, from_west.get(), quads.shape[1])
    tokens[grid.own_rows :, :] = west_tokens
    windowed = dot(to_windows.get()[...], tokens[...])
    normed, inverse_std = normalize(windowed)
    rolled = normed.astype(jnp.bfloat16)
    normed_out.ref[...] = normed
    normed_out.send()
    std_out.ref[...] = inverse_std
    std_out.send()
    projected[...] = dot(rolled, attend_weight.get()[...]).astype(jnp.bfloat16)
    mask_all = head_mask.get()[...]
    bias_ref, mask_ref = bias.get(), mask.get()

    def heads_of(rows, part, group):
        first = part * channels + group * LANES
        return projected[rows, first : first + LANES]

    def forward(window, carry):
        rows = pl.ds(pl.multiple_of(window * SLOT, SLOT), SLOT)
        extra = mask_ref[window // grid.across]
        for group in range(groups):
            lanes = group * LANES
            query, key, value = [heads_of(rows, part, group) for part in range(3)]
            spread_query = jnp.concatenate([query] * per_group, 0) * mask_all
            scores = dot_t(key, spread_query) * scale + bias_ref[group] + extra
            weights = jnp.exp(scores - jnp.max(scores, 0, keepdims=True))
            prob = weights / jnp.sum(weights, 0, keepdims=True)
            probs[window * groups + group] = prob
            mixed = dot(prob.astype(jnp.bfloat16).T, value)
            attended[rows, lanes : lanes + LANES] = head_sum(mixed, mask_all, per_group).astype(jnp.bfloat16)
        return carry

    lax.fori_loop(0, grid.windows, forward, 0)

    spread(quads, cot.get(), grid.cot_stride)
    quads[grid.cot_own :, :] = west_quads
    select = to_quads.get()[...]
    attended_quads = pick(select, attended[...])
    feature_quads = dot(select, windowed.astype(jnp.bfloat16))
    branch = dot(attended_quads, output_weight.get()[...])
    hidden = (feature_quads + branch).astype(jnp.bfloat16).astype(jnp.float32)
    count = grid.quad_count
    phases = [hidden[k * count : (k + 1) * count] for k in range(4)]
    width = 4 * channels
    mean = sum(jnp.sum(phase, -1, keepdims=True) for phase in phases) / width
    centred = [phase - mean for phase in phases]
    variance = sum(jnp.sum(phase * phase, -1, keepdims=True) for phase in centred) / width
    quad_std = lax.rsqrt(variance + EPS)
    quad_normed = [phase * quad_std for phase in centred]
    cot_quads = pick(cot_to_quads.get()[...], quads[...])
    merge_ref = merge_weight.get()
    quad_grads = []
    for k in range(4):
        quad16_out.ref[k * count : (k + 1) * count, :] = quad_normed[k].astype(jnp.bfloat16)
        quad_grads.append(dot_t(cot_quads, merge_ref[k * channels : (k + 1) * channels, :]))
    quad16_out.send()
    first = sum(jnp.sum(part, -1, keepdims=True) for part in quad_grads) / width
    second = sum(jnp.sum(part * n, -1, keepdims=True) for part, n in zip(quad_grads, quad_normed)) / width
    hidden_grad = jnp.concatenate(
        [quad_std * (part - first - n * second) for part, n in zip(quad_grads, quad_normed)], 0
    ).astype(jnp.bfloat16)
    branch_grad = pick(from_quads.get()[...], hidden_grad)
    branch_grad_out.ref[...] = branch_grad
    branch_grad_out.send()
    outer[...] = dot_t(branch_grad, output_weight.get()[...]).astype(jnp.bfloat16)
    projected_grad = projected_grad_out.ref

    def backward(window, carry):
        rows = pl.ds(pl.multiple_of(window * SLOT, SLOT), SLOT)
        for group in range(groups):
            lanes = group * LANES
            query, key, value = [heads_of(rows, part, group) for part in range(3)]
            grads = outer[rows, lanes : lanes + LANES]
            spread_query = jnp.concatenate([query] * per_group, 0) * mask_all
            spread_grads = jnp.concatenate([grads] * per_group, 0) * mask_all
            prob = probs[window * groups + group]
            value_grad = dot(prob.astype(jnp.bfloat16), spread_grads)
            score_grad = dot_t(value, spread_grads)
            inner = jnp.sum(prob * score_grad, 0, keepdims=True)
            soft = (prob * (score_grad - inner) * scale).astype(jnp.bfloat16)
            key_grad = dot(soft, spread_query)
            query_grad = head_sum(dot(soft.T, key), mask_all, per_group)
            for part, grad in enumerate((query_grad, key_grad, value_grad)):
                at = part * channels + lanes
                projected_grad[rows, at : at + LANES] = grad.astype(jnp.bfloat16)
        return carry

    lax.fori_loop(0, grid.windows, backward, 0)
    projected_grad_out.send()

    columns = lax.broadcasted_iota(jnp.int32, (channels, channels), 1)
    half, split = channels // 2, 2 * channels
    for route, ref in enumerate((order_a, order_b)):
        order = jnp.where(columns == ref.get()[...], 1.0, 0.0).astype(jnp.bfloat16)
        rolled_t = dot_t(order, rolled).astype(jnp.bfloat16)
        if route == 0:
            pieces = [(0, dot(rolled_t, projected_grad[:, :split]))]
        else:
            attended_t = dot_t(order, attended[...]).astype(jnp.bfloat16)
            pieces = [
                (split, dot(rolled_t, projected_grad[:, split:])),
                (3 * channels, dot(attended_t, branch_grad)),
            ]
        for at, piece in pieces:
            piece = piece.astype(jnp.bfloat16)
            kept.ref[:, at : at + piece.shape[1]] = piece[:half]
            sent.ref[:, at : at + piece.shape[1]] = piece[half:]
    kept.send()
    sent.send()


def tail_kernel(
    grid, projected_grad, attend_weight, normed, inverse_std, branch_grad, tokens_back, quad16, merge_weight,
    quads_back, back, feature_grads, merged,
):
    channels = grid.channels
    grads = dot_t(projected_grad.get()[...], attend_weight.get()[...])
    n = normed.get()[...]
    first = jnp.mean(grads, -1, keepdims=True)
    second = jnp.mean(grads * n, -1, keepdims=True)
    rolled_grad = inverse_std.get()[...] * (grads - first - n * second)
    total = (branch_grad.get()[...].astype(jnp.float32) + rolled_grad).astype(jnp.bfloat16)
    feature_grads.ref[...] = total
    feature_grads.send()
    count = grid.quad_count
    sums = None
    quad_ref, merge_ref = quad16.get(), merge_weight.get()
    for k in range(4):
        term = dot(quad_ref[k * count : (k + 1) * count, :], merge_ref[k * channels : (k + 1) * channels, :])
        sums = term if sums is None else sums + term
    sums = sums.astype(jnp.bfloat16)
    merged.ref[...] = sums
    merged.send()
    pack(grid, back.ref, pick(tokens_back.get()[...], total), pick(quads_back.get()[...], sums))
    back.send()


def last_kernel(grid, feature_grads, merged, came, final_tokens, final_quads, out, merged_out):
    width = merged_out.ref.shape[2]
    tokens, quads = unpack(grid, came.get(), width)
    rows = grid.window_rows
    select = final_tokens.get()
    total = dot(select[:, :rows], feature_grads.get()[...]) + dot(select[:, rows:], tokens)
    for line in range(grid.rows):
        out.ref[line] = total[line * grid.stride : line * grid.stride + grid.cols].astype(jnp.bfloat16)
    out.send()
    select = final_quads.get()
    count = grid.quad_count
    sums = dot(select[:, :count], merged.get()[...]) + dot(select[:, count:], quads)
    for line in range(grid.quad_lines):
        first = line * grid.quad_stride
        merged_out.ref[line] = sums[first : first + grid.quad_cols].astype(jnp.bfloat16)
    merged_out.send()


class Operand:
    def __init__(self, source, ref, sem):
        self.ref, self.copy, self.waited = ref, pltpu.make_async_copy(source, ref, sem), False
        self.copy.start()

    def get(self):
        if not self.waited:
            self.copy.wait()
            self.waited = True
        return self.ref


class Result:
    def __init__(self, target, ref, sem):
        self.ref, self.copy = ref, pltpu.make_async_copy(ref, target, sem)

    def send(self):
        self.copy.start()


def call(kernel, outs, *args, scratch=(), name):
    def body(*refs):
        counts = len(args), len(outs)
        given, refs = refs[: counts[0]], refs[counts[0] :]
        made, refs = refs[: counts[1]], refs[counts[1] :]
        inner, refs = refs[: len(scratch)], refs[len(scratch) :]
        buffers, sems = refs[:-1], refs[-1]
        operands = [Operand(g, buffers[i], sems.at[i]) for i, g in enumerate(given)]
        results = [
            Result(m, buffers[counts[0] + i], sems.at[counts[0] + i]) for i, m in enumerate(made)
        ]
        kernel(*operands, *results, *inner)
        for operand in operands:
            operand.get()
        for result in results:
            result.copy.wait()

    anywhere = pl.BlockSpec(memory_space=pl.ANY)
    buffers = [pltpu.VMEM(a.shape, a.dtype) for a in (*args, *outs)]
    return pl.pallas_call(
        body,
        out_shape=outs,
        in_specs=[anywhere] * len(args),
        out_specs=[anywhere] * len(outs),
        scratch_shapes=[*scratch, *buffers, pltpu.SemaphoreType.DMA((len(args) + len(outs),))],
        compiler_params=pltpu.CompilerParams(vmem_limit_bytes=56 * 2**20),
        name=name,
    )(*args)


def f32(*shape):
    return jax.ShapeDtypeStruct(shape, jnp.float32)


def b16(*shape):
    return jax.ShapeDtypeStruct(shape, jnp.bfloat16)


def window_bias(position_bias, grid):
    place = np.arange(SLOT)
    row, col = place // (WINDOW + 1), place % (WINDOW + 1)
    real = (row < WINDOW) & (col < WINDOW)
    span = 2 * WINDOW - 1
    index = (row[None, :] - row[:, None] + WINDOW - 1) * span + (col[None, :] - col[:, None] + WINDOW - 1)
    index = np.where(real[:, None] & real[None, :], index, 0)
    one_hot = jnp.asarray(index.reshape(-1)[:, None] == np.arange(span * span)[None, :]).astype(jnp.float32)
    heads = grid.heads
    values = jnp.dot(one_hot, position_bias, precision=lax.Precision.HIGHEST)
    per_group = LANES // (grid.channels // heads)
    values = values.reshape(SLOT, SLOT, heads // per_group, per_group).transpose(2, 0, 3, 1)
    values = values.reshape(heads // per_group, SLOT, per_group * SLOT)
    padded = jnp.asarray(np.where(real, 0.0, -1e30), jnp.float32)
    values = values + padded[None, :, None]
    line = np.arange(grid.bands)[:, None] * WINDOW + row[None, :]
    region = (line >= grid.rows - WINDOW).astype(int) + (line >= grid.rows - SHIFT).astype(int)
    blocked = np.where(region[:, :, None] == region[:, None, :], 0.0, -100.0)
    blocked = np.where(real[:, None] & real[None, :], blocked, 0.0)
    mask = jnp.asarray(np.concatenate([blocked] * per_group, 2), jnp.float32)
    return values, mask


def halving_bits():
    frame_bits = lax.axis_size("frame").bit_length() - 1
    azim_bits = lax.axis_size("azim").bit_length() - 1
    frame = [("frame", bit, 1 << bit) for bit in range(frame_bits)]
    azim = [("azim", bit, 1 << (bit + frame_bits)) for bit in range(azim_bits)]
    rest = frame[2:] + azim[1:]
    return [frame[:1] + azim[:1] + frame[1:2] + rest, frame[:2] + azim[:1] + rest]


def exchange(block, axis, bit):
    return lax.ppermute(block, axis, [(i, i ^ (1 << bit)) for i in range(lax.axis_size(axis))])


def row_orders(channels):
    orders = []
    for bits in halving_bits():
        members = 1 << len(bits)
        row = np.arange(channels)
        if channels % members:
            orders.append(jnp.asarray(row, jnp.int32)[:, None])
            continue
        each = channels // members
        piece = jnp.zeros(channels, jnp.int32)
        for stage, (axis, bit, weight) in enumerate(bits):
            far = (row // each >> (len(bits) - 1 - stage)) & 1
            own = (lax.axis_index(axis) >> bit) & 1
            piece = piece + (own ^ jnp.asarray(far, jnp.int32)) * weight
        orders.append((piece * each + jnp.asarray(row % each, jnp.int32))[:, None])
    return orders


def scatter_flat(terms):
    bits = halving_bits()[0]
    members = 1 << len(bits)
    widths = [term.size // members for term in terms]
    held = jnp.concatenate([term.reshape(members, -1) for term in terms], 1)
    held = held.reshape((2,) * len(bits) + (-1,))
    for axis, bit, weight in bits:
        dim = len(bits) - weight.bit_length()
        own = (lax.axis_index(axis) >> bit) & 1
        kept = lax.dynamic_slice_in_dim(held, own, 1, dim)
        got = exchange(lax.dynamic_slice_in_dim(held, 1 - own, 1, dim), axis, bit)
        total = kept.astype(jnp.float32) + got.astype(jnp.float32)
        held = total.astype(jnp.bfloat16)
    total = total.reshape(-1)
    return total[: widths[0]], total[widths[0] :]


def halve(total):
    held, half = total.astype(jnp.bfloat16), total.shape[0] // 2
    return held[:half], held[half:]


def add(kept, got):
    return kept.astype(jnp.float32) + got.astype(jnp.float32)


def scatter_sum(kept, sent, channels):
    routes = halving_bits()
    if channels % (1 << len(routes[0])):
        whole = jnp.concatenate([kept, sent], 0)
        return scatter_flat((whole[:, : 3 * channels], whole[:, 3 * channels :]))
    got = exchange(sent, *routes[0][0][:2])
    split = 2 * channels
    parts = [add(kept[:, :split], got[:, :split]), add(kept[:, split:], got[:, split:])]
    for stage in (1, 2):
        halves = [halve(part) for part in parts]
        gots = [exchange(sent, *bits[stage][:2]) for (_, sent), bits in zip(halves, routes)]
        parts = [add(kept, got) for (kept, _), got in zip(halves, gots)]
    total = jnp.concatenate(parts, 1)
    for axis, bit, _ in routes[0][3:]:
        kept, sent = halve(total)
        total = add(kept, exchange(sent, axis, bit))
    return total[:, : 3 * channels].reshape(-1), total[:, 3 * channels :].reshape(-1)


def from_behind(block, axis, distance):
    size = lax.axis_size(axis)
    return lax.ppermute(block, axis, [((i - distance) % size, i) for i in range(size)])


def per_device(features, position_bias, attend_weight, output_weight, merge_weight, cotangent):
    x, cot = features[0], cotangent[0]
    rows, cols, channels = x.shape
    heads = position_bias.shape[1]
    grid = Grid(rows, cols, heads, channels)
    width = cot.shape[2]
    bf16 = jnp.bfloat16
    halo_rows = grid.west_rows + width // channels * grid.cot_halo
    own, quads = grid.window_rows, 4 * grid.quad_count
    (to_next,) = call(
        functools.partial(pre_kernel, grid), (b16(halo_rows, channels),),
        x, cot, grid.pack_tokens(), grid.pack_cot(), name="pack",
        scratch=[pltpu.VMEM((grid.own_rows, channels), bf16), pltpu.VMEM((grid.cot_own, width), bf16)],
    )
    from_west = from_behind(to_next, "azim", 1)
    bias, mask = window_bias(position_bias, grid)
    per_group = LANES * heads // channels
    lane_head = np.arange(LANES) // (channels // heads)
    head_mask = jnp.asarray(np.repeat(np.arange(per_group), SLOT)[:, None] == lane_head[None, :]).astype(bf16)
    half = channels // 2
    kept, sent, projected_grad, normed, inverse_std, branch_grad, quad16 = call(
        functools.partial(main_kernel, grid),
        (
            b16(half, 4 * channels), b16(half, 4 * channels), b16(own, 3 * channels), f32(own, channels),
            f32(own, 1), b16(own, channels), b16(quads, channels),
        ),
        x, from_west, grid.to_windows(), attend_weight, head_mask, bias, mask, grid.to_quads(), output_weight, cot,
        grid.cot_to_quads(), merge_weight, grid.from_quads(), *row_orders(channels), name="attend",
        scratch=[
            pltpu.VMEM((grid.own_rows + grid.west_rows, channels), bf16),
            pltpu.VMEM((grid.cot_own + grid.cot_halo, width), bf16),
            pltpu.VMEM((own, 3 * channels), bf16),
            pltpu.VMEM((own, channels), bf16),
            pltpu.VMEM((grid.windows * heads // per_group, SLOT, per_group * SLOT), jnp.float32),
            pltpu.VMEM((own, channels), bf16),
        ],
    )
    back, feature_grads, merged_quads = call(
        functools.partial(tail_kernel, grid),
        (b16(halo_rows, channels), b16(own, channels), b16(grid.quad_count, width)),
        projected_grad, attend_weight, normed, inverse_std, branch_grad, grid.tokens_back(), quad16, merge_weight,
        grid.quads_back(), name="tail",
    )
    came = from_behind(back, "azim", -1)
    feature_grad, merged = call(
        functools.partial(last_kernel, grid),
        (b16(rows, cols, channels), b16(grid.quad_lines, grid.quad_cols, width)),
        feature_grads, merged_quads, came, grid.final_tokens(), grid.final_quads(), name="last",
    )
    attend_grad, output_grad = scatter_sum(kept, sent, channels)
    return (merged[None], feature_grad[None], attend_grad, output_grad)


def solution(mesh):
    in_specs = (P("frame", None, "azim", None), P(), P(), P(), P(), P("frame", None, "azim", None))
    out_specs = (
        P("frame", None, "azim", None),
        P("frame", None, "azim", None),
        P(("azim", "frame")),
        P(("azim", "frame")),
    )
    return jax.shard_map(
        per_device, mesh=mesh, in_specs=in_specs, out_specs=out_specs, check_vma=False
    )
```

```python
import functools

import jax
import jax.numpy as jnp
import numpy as np
from jax import lax
from jax.experimental import pallas as pl
from jax.experimental.pallas import tpu as pltpu
from jax.sharding import PartitionSpec as P


WINDOW = 7
SHIFT = 3
SLOT = 64
LANES = 128
EPS = 1e-05


def up(value, step):
    return -(-value // step) * step


def dot(left, right):
    return lax.dot_general(left, right, (((1,), (0,)), ((), ())), preferred_element_type=jnp.float32)


def dot_t(left, right):
    return lax.dot_general(left, right, (((1,), (1,)), ((), ())), preferred_element_type=jnp.float32)


def pick(select, values):
    return dot(select, values).astype(jnp.bfloat16)


class Grid:
    def __init__(self, rows, cols, heads, channels):
        self.rows, self.cols, self.heads, self.channels = rows, cols, heads, channels
        self.west = WINDOW - SHIFT
        self.last = cols - self.west
        self.bands, self.across = rows // WINDOW, cols // WINDOW
        self.windows = self.bands * self.across
        self.local_windows = self.windows - self.bands
        self.window_rows, self.local_rows = self.windows * SLOT, self.local_windows * SLOT
        self.stride = up(cols, 16)
        self.own_rows = rows * self.stride
        self.west_rows = up(rows * self.west, 16)
        self.quad_lines, self.quad_cols, self.quad_west = rows // 2, cols // 2, self.west // 2
        self.quad_stride = up(self.quad_cols, 8)
        self.quad_count = up(self.quad_lines * self.quad_stride, 16)
        self.cot_stride = up(self.quad_cols, 16)
        self.cot_own = self.quad_lines * self.cot_stride
        self.cot_halo = up(self.quad_west * self.quad_lines, 16)

    def source(self, row, col):
        return row * self.stride + col if col >= 0 else self.own_rows + row * self.west + col + self.west

    def window_row(self, row, col):
        line = (row - SHIFT) % self.rows
        across, place = divmod(col + self.west, WINDOW)
        window = (across - 1) % self.across * self.bands + line // WINDOW
        return window * SLOT + line % WINDOW * (WINDOW + 1) + place

    def quad_row(self, row, col):
        phase = 2 * (col % 2) + row % 2
        return phase * self.quad_count + row // 2 * self.quad_stride + (col + self.west) // 2

    def onehot(self, shape, pairs):
        out = np.zeros(shape, np.float32)
        for i, j in pairs:
            out[i, j] = 1
        return jnp.asarray(out, jnp.bfloat16)

    def cells(self, first, last):
        return [(r, c) for r in range(self.rows) for c in range(first, last)]

    def to_windows(self):
        pairs = [(self.window_row(r, c), self.source(r, c)) for r, c in self.cells(-self.west, self.last)]
        return self.onehot((self.window_rows, self.own_rows + self.west_rows), pairs)

    def to_quads(self):
        pairs = [(self.quad_row(r, c), self.window_row(r, c)) for r, c in self.cells(-self.west, self.last)]
        return self.onehot((4 * self.quad_count, self.window_rows), pairs)

    def from_quads(self):
        return self.to_quads().T

    def pack_tokens(self):
        pairs = [
            (r * self.west + c - self.last, self.source(r, c)) for r, c in self.cells(self.last, self.cols)
        ]
        return self.onehot((self.west_rows, self.own_rows), pairs)

    def quad_cells(self, first, last):
        return [(i, j) for i in range(self.quad_lines) for j in range(first, last)]

    def pack_cot(self):
        first = self.quad_cols - self.quad_west
        pairs = [
            (self.quad_west * i + j - first, i * self.cot_stride + j)
            for i, j in self.quad_cells(first, self.quad_cols)
        ]
        return self.onehot((self.cot_halo, self.cot_own), pairs)

    def cot_to_quads(self):
        pairs = [
            (i * self.quad_stride + j, self.cot_own + self.quad_west * i + j)
            for i, j in self.quad_cells(0, self.quad_west)
        ]
        pairs += [
            (i * self.quad_stride + j, i * self.cot_stride + j - self.quad_west)
            for i, j in self.quad_cells(self.quad_west, self.quad_cols)
        ]
        return self.onehot((self.quad_count, self.cot_own + self.cot_halo), pairs)

    def tokens_back(self):
        pairs = [(r * self.west + c + self.west, self.window_row(r, c)) for r, c in self.cells(-self.west, 0)]
        return self.onehot((self.west_rows, self.window_rows), pairs)

    def quads_back(self):
        pairs = [
            (self.quad_west * i + j, i * self.quad_stride + j) for i, j in self.quad_cells(0, self.quad_west)
        ]
        return self.onehot((self.cot_halo, self.quad_count), pairs)

    def final_tokens(self):
        pairs = [(self.source(r, c), self.window_row(r, c)) for r, c in self.cells(0, self.last)]
        pairs += [
            (self.source(r, c), self.window_rows + r * self.west + c - self.last)
            for r, c in self.cells(self.last, self.cols)
        ]
        return self.onehot((self.own_rows, self.window_rows + self.west_rows), pairs)

    def final_quads(self):
        first = self.quad_cols - self.quad_west
        pairs = [
            (i * self.quad_stride + j, i * self.quad_stride + j + self.quad_west)
            for i, j in self.quad_cells(0, first)
        ]
        pairs += [
            (i * self.quad_stride + j, self.quad_count + self.quad_west * i + j - first)
            for i, j in self.quad_cells(first, self.quad_cols)
        ]
        return self.onehot((self.quad_count, self.quad_count + self.cot_halo), pairs)


def normalize(values):
    centred = values - jnp.mean(values, -1, keepdims=True)
    inverse_std = lax.rsqrt(jnp.mean(centred * centred, -1, keepdims=True) + EPS)
    return centred * inverse_std, inverse_std


def spread(ref, grid_ref, stride):
    ref[0 : grid_ref.shape[0] * stride, :] = jnp.zeros((grid_ref.shape[0] * stride, ref.shape[1]), ref.dtype)
    for line in range(grid_ref.shape[0]):
        ref[line * stride : line * stride + grid_ref.shape[1], :] = grid_ref[line]


def pack(grid, out, tokens, quads):
    out[0 : grid.west_rows, :] = tokens
    for part in range(quads.shape[1] // grid.channels):
        first = grid.west_rows + part * grid.cot_halo
        out[first : first + grid.cot_halo, :] = quads[:, part * grid.channels : (part + 1) * grid.channels]


def unpack(grid, ref, width):
    first = grid.west_rows
    parts = [
        ref[first + part * grid.cot_halo : first + (part + 1) * grid.cot_halo, :]
        for part in range(width // grid.channels)
    ]
    return ref[0 : grid.west_rows, :], jnp.concatenate(parts, 1)


def pre_kernel(grid, x, cot, pack_tokens, pack_cot, to_next, tokens, quads):
    spread(tokens, x.get(), grid.stride)
    spread(quads, cot.get(), grid.cot_stride)
    halo = pick(pack_cot.get()[...], quads[...])
    pack(grid, to_next.ref, pick(pack_tokens.get()[...], tokens[...]), halo)
    to_next.send()


def build_bias(grid, table, bias, mask):
    span, count = 2 * WINDOW - 1, WINDOW + 1
    per_group = LANES * grid.heads // grid.channels
    center = (WINDOW - 1) * span + WINDOW - 1
    rows = table.shape[1]
    values = jnp.concatenate([table[...], jnp.zeros((table.shape[0], 2 * LANES - rows), jnp.float32)], 1)
    key = lax.broadcasted_iota(jnp.int32, (SLOT, per_group * SLOT), 0)
    query = lax.broadcasted_iota(jnp.int32, (SLOT, per_group * SLOT), 1) & (SLOT - 1)
    key_row, key_col = key >> 3, key & (count - 1)
    query_row = query >> 3
    padded = jnp.where((key_row < WINDOW) & (key_col < WINDOW), 0.0, -1e30)
    key_late = (key_row >= WINDOW - SHIFT).astype(jnp.int32)
    query_late = (query_row >= WINDOW - SHIFT).astype(jnp.int32)
    mask[...] = jnp.where(key_late != query_late, -100.0, 0.0)
    place = lax.broadcasted_iota(jnp.int32, (LANES, per_group * SLOT), 0)
    lane = lax.broadcasted_iota(jnp.int32, (LANES, per_group * SLOT), 1)
    inside = lane & (SLOT - 1)
    wanted = (inside >> 3) * span + (inside & (count - 1))
    hit = (place == wanted) & ((inside >> 3) < WINDOW) & ((inside & (count - 1)) < WINDOW)
    for group in range(grid.heads // per_group):
        total = padded
        for head in range(per_group):
            line = jnp.broadcast_to(values[group * per_group + head : group * per_group + head + 1], (count, 2 * LANES))
            line = pltpu.roll(line, 0, 1, stride=1, stride_axis=0)
            blocks = [
                pltpu.roll(line, (span * r - center) % (2 * LANES), 1)[:, :LANES] for r in range(WINDOW)
            ]
            blocks.append(jnp.zeros((count, LANES), jnp.float32))
            block = jnp.concatenate(blocks, 0)
            high = block.astype(jnp.bfloat16)
            low = (block - high.astype(jnp.float32)).astype(jnp.bfloat16)
            select = jnp.where(hit & ((lane // SLOT) == head), 1.0, 0.0).astype(jnp.bfloat16)
            total = total + dot(high, select) + dot(low, select)
        bias[group] = total


class Heads:
    def __init__(self, grid, head_mask):
        self.channels = grid.channels
        self.head_size = grid.channels // grid.heads
        self.scale = self.head_size ** (-0.5)
        self.per_group = LANES // self.head_size
        self.groups = grid.heads // self.per_group
        self.head_mask = head_mask

    def spread(self, values):
        return jnp.concatenate([values] * self.per_group, 0) * self.head_mask

    def collect(self, stacked):
        total = None
        for head in range(self.per_group):
            part = stacked[head * SLOT : (head + 1) * SLOT, :]
            part = jnp.where(self.head_mask[head * SLOT : (head + 1) * SLOT, :] > 0, part, 0.0)
            total = part if total is None else total + part
        return total

    def split(self, projected, window, group):
        rows = slice(window * SLOT, (window + 1) * SLOT)
        firsts = [part * self.channels + group * LANES for part in range(3)]
        return [projected[rows, first : first + LANES] for first in firsts]

    def forward(self, jobs, fillers=()):
        def product(job):
            query, key, value = self.split(job.projected, job.window, job.group)
            return dot_t(key, self.spread(query)), value

        def soften(job, scores, value):
            scores = scores * self.scale + job.bias[job.group]
            if job.extra is not None:
                scores = scores + job.extra[...]
            weights = jnp.exp(scores - jnp.max(scores, 0, keepdims=True))
            prob = weights / jnp.sum(weights, 0, keepdims=True)
            job.probs[job.window * self.groups + job.group] = prob
            return prob.astype(jnp.bfloat16), value

        def mix(job, prob, value):
            return (dot(prob.T, value),)

        def store(job, mixed):
            rows, lanes = job.window * SLOT, job.group * LANES
            job.attended[rows : rows + SLOT, lanes : lanes + LANES] = self.collect(mixed).astype(jnp.bfloat16)
            return ()

        interleave(jobs, (product, soften, mix, store), fillers)

    def backward(self, jobs, outer, projected_grad, fillers=()):
        def rows_of(job):
            return slice(job.first + job.window * SLOT, job.first + (job.window + 1) * SLOT)

        def put(job, part, grad):
            at = part * self.channels + job.group * LANES
            projected_grad[rows_of(job), at : at + LANES] = grad.astype(jnp.bfloat16)

        def product(job):
            value = self.split(job.projected, job.window, job.group)[2]
            grads = self.spread(outer[rows_of(job), job.group * LANES : (job.group + 1) * LANES])
            prob = job.probs[job.window * self.groups + job.group]
            put(job, 2, dot(prob.astype(jnp.bfloat16), grads))
            return (dot_t(value, grads),)

        def soften(job, score_grad):
            prob = job.probs[job.window * self.groups + job.group]
            inner = jnp.sum(prob * score_grad, 0, keepdims=True)
            return ((prob * (score_grad - inner) * self.scale).astype(jnp.bfloat16),)

        def mix(job, soft):
            query, key, _ = self.split(job.projected, job.window, job.group)
            put(job, 1, dot(soft, self.spread(query)))
            return (dot(soft.T, key),)

        def store(job, mixed):
            put(job, 0, self.collect(mixed))
            return ()

        interleave(jobs, (product, soften, mix, store), fillers)


class Job:
    def __init__(self, **fields):
        self.__dict__.update(fields)


def jobs_of(windows, groups, **fields):
    return [Job(window=window, group=group, **fields) for window in range(windows) for group in range(groups)]


def interleave(jobs, stages, fillers=()):
    states = [()] * len(jobs)
    fillers = list(fillers)
    for turn in range(len(jobs) + len(stages) - 1):
        for depth, stage in reversed(list(enumerate(stages))):
            at = turn - depth
            if 0 <= at < len(jobs):
                states[at] = stage(jobs[at], *states[at])
        if fillers:
            fillers.pop(0)()
    for filler in fillers:
        filler()


def with_masks(jobs, grid, mask):
    for job in jobs:
        job.extra = mask if job.window % grid.bands == grid.bands - 1 else None
    return jobs


def local_kernel(grid, x, cot, table, to_windows, attend_weight, head_mask, *rest):
    tokens = rest[-1]
    bias, mask, quads, windowed, normed, std, projected, attended, probs, orders, rolled_t, attended_t = [
        r.ref for r in rest[-13:-1]
    ]
    spread(quads, cot.get(), grid.cot_stride)
    spread(tokens, x.get(), grid.stride)
    build_bias(grid, table.get(), bias, mask)
    values = dot(to_windows.get()[:, : grid.own_rows], tokens[...])
    windowed[...] = values
    local = grid.local_rows
    n, inverse_std = normalize(values[:local])
    normed[...] = n
    std[...] = inverse_std
    projected[...] = dot(n.astype(jnp.bfloat16), attend_weight.get()[...]).astype(jnp.bfloat16)
    heads = Heads(grid, head_mask.get()[...])
    jobs = jobs_of(
        grid.local_windows, heads.groups, projected=projected, bias=bias, attended=attended, probs=probs
    )
    heads.forward(with_masks(jobs, grid, mask))
    rolled = n.astype(jnp.bfloat16)
    order = row_order(grid.channels)
    orders[...] = order
    rolled_t[...] = dot_t(order, rolled).astype(jnp.bfloat16)
    attended_t[...] = dot_t(order, attended[...]).astype(jnp.bfloat16)


def main_kernel(
    grid, from_west, to_windows, attend_weight, head_mask, bias, mask, to_quads, output_weight,
    cot_to_quads, merge_weight, from_quads, quads, windowed_own, normed_local, std_local, projected_local,
    attended_local, probs_local, orders, rolled_t_local, attended_t_local,
    kept, sent, projected_grad_out, normed_out, std_out, branch_grad_out, quad16_out,
    projected, attended, probs, outer, quad_grads, rolled_t, attended_t,
):
    channels, local = grid.channels, grid.local_rows
    west_tokens, west_quads = unpack(grid, from_west.get(), quads.ref.shape[1])
    windowed = windowed_own.ref[...] + dot(to_windows.ref[:, grid.own_rows :], west_tokens)
    normed, inverse_std = normalize(windowed[local:])
    normed_out.ref[:local] = normed_local.ref[...]
    normed_out.ref[local:] = normed
    std_out.ref[:local] = std_local.ref[...]
    std_out.ref[local:] = inverse_std
    projected[...] = dot(normed.astype(jnp.bfloat16), attend_weight.ref[...]).astype(jnp.bfloat16)
    rolled = normed.astype(jnp.bfloat16)
    cot_select = cot_to_quads.ref
    cot_quads = dot(cot_select[:, : grid.cot_own], quads.ref[: grid.cot_own, :])
    cot_quads = (cot_quads + dot(cot_select[:, grid.cot_own :], west_quads)).astype(jnp.bfloat16)
    merge_ref = merge_weight.ref

    def quad_product(k):
        quad_grads[k] = dot_t(cot_quads, merge_ref[k * channels : (k + 1) * channels, :])

    heads = Heads(grid, head_mask.ref[...])
    jobs = jobs_of(grid.bands, heads.groups, projected=projected, bias=bias.ref, attended=attended, probs=probs)
    heads.forward(
        with_masks(jobs, grid, mask.ref), [functools.partial(quad_product, k) for k in range(4)]
    )

    select = to_quads.ref
    attended_quads = (
        dot(select[:, :local], attended_local.ref[...]) + dot(select[:, local:], attended[...])
    ).astype(jnp.bfloat16)
    feature_quads = dot(select[...], windowed.astype(jnp.bfloat16))
    branch = dot(attended_quads, output_weight.ref[...])
    hidden = (feature_quads + branch).astype(jnp.bfloat16).astype(jnp.float32)
    count = grid.quad_count
    phases = [hidden[k * count : (k + 1) * count] for k in range(4)]
    width = 4 * channels
    mean = sum(jnp.sum(phase, -1, keepdims=True) for phase in phases) / width
    centred = [phase - mean for phase in phases]
    variance = sum(jnp.sum(phase * phase, -1, keepdims=True) for phase in centred) / width
    quad_std = lax.rsqrt(variance + EPS)
    quad_normed = [phase * quad_std for phase in centred]
    for k in range(4):
        quad16_out.ref[k * count : (k + 1) * count, :] = quad_normed[k].astype(jnp.bfloat16)
    first = sum(jnp.sum(quad_grads[k], -1, keepdims=True) for k in range(4)) / width
    second = sum(jnp.sum(quad_grads[k] * quad_normed[k], -1, keepdims=True) for k in range(4)) / width
    hidden_grad = jnp.concatenate(
        [quad_std * (quad_grads[k] - first - quad_normed[k] * second) for k in range(4)], 0
    ).astype(jnp.bfloat16)
    branch_grad = pick(from_quads.ref[...], hidden_grad)
    branch_grad_out.ref[...] = branch_grad
    outer[...] = dot_t(branch_grad, output_weight.ref[...]).astype(jnp.bfloat16)
    projected_grad = projected_grad_out.ref
    jobs = jobs_of(
        grid.local_windows, heads.groups, projected=projected_local.ref, probs=probs_local.ref, first=0
    )
    jobs += jobs_of(grid.bands, heads.groups, projected=projected, probs=probs, first=local)

    def turned():
        rolled_t[...] = dot_t(orders.ref[...], rolled).astype(jnp.bfloat16)

    def turned_attended():
        attended_t[...] = dot_t(orders.ref[...], attended[...]).astype(jnp.bfloat16)

    heads.backward(jobs, outer, projected_grad, [turned_attended, turned])

    half, joint = channels // 2, 3 * channels

    def put(first, local_t, halo_t, grads):
        piece = dot(local_t, grads[:local]) + dot(halo_t, grads[local:])
        kept.ref[:, first : first + piece.shape[1]] = piece[:half]
        sent.ref[:, first : first + piece.shape[1]] = piece[half:].astype(jnp.bfloat16)

    put(joint, attended_t_local.ref[...], attended_t[...], branch_grad)
    for first in range(0, joint, channels):
        put(first, rolled_t_local.ref[...], rolled_t[...], projected_grad[:, first : first + channels])


def tail_kernel(
    grid, projected_grad, attend_weight, normed, inverse_std, branch_grad, quads_back, tokens_back, merged,
    back, feature_grads,
):
    grads = dot_t(projected_grad.get()[...], attend_weight.get()[...])
    n = normed.get()[...]
    first = jnp.mean(grads, -1, keepdims=True)
    second = jnp.mean(grads * n, -1, keepdims=True)
    rolled_grad = inverse_std.get()[...] * (grads - first - n * second)
    total = (branch_grad.get()[...].astype(jnp.float32) + rolled_grad).astype(jnp.bfloat16)
    feature_grads.ref[...] = total
    feature_grads.send()
    pack(grid, back.ref, pick(tokens_back.get()[...], total), pick(quads_back.get()[...], merged.get()[...]))
    back.send()


def merge_kernel(grid, quad16, merge_weight, merged):
    channels, count = grid.channels, grid.quad_count
    sums = None
    quad_ref, merge_ref = quad16.get(), merge_weight.get()
    for k in range(4):
        term = dot(quad_ref[k * count : (k + 1) * count, :], merge_ref[k * channels : (k + 1) * channels, :])
        sums = term if sums is None else sums + term
    merged.ref[...] = sums.astype(jnp.bfloat16)
    merged.send()


def last_kernel(grid, feature_grads, merged, came, final_tokens, final_quads, out, merged_out):
    width = merged_out.ref.shape[2]
    tokens, quads = unpack(grid, came.get(), width)
    rows = grid.window_rows
    select = final_tokens.get()
    total = dot(select[:, :rows], feature_grads.get()[...]) + dot(select[:, rows:], tokens)
    for line in range(grid.rows):
        out.ref[line] = total[line * grid.stride : line * grid.stride + grid.cols].astype(jnp.bfloat16)
    out.send()
    select = final_quads.get()
    count = grid.quad_count
    sums = dot(select[:, :count], merged.get()[...]) + dot(select[:, count:], quads)
    for line in range(grid.quad_lines):
        first = line * grid.quad_stride
        merged_out.ref[line] = sums[first : first + grid.quad_cols].astype(jnp.bfloat16)
    merged_out.send()


class Operand:
    def __init__(self, source, ref, sem):
        self.ref, self.copy, self.waited = ref, pltpu.make_async_copy(source, ref, sem), False
        self.copy.start()

    def get(self):
        if not self.waited:
            self.copy.wait()
            self.waited = True
        return self.ref


class Result:
    def __init__(self, target, ref, sem):
        self.ref, self.copy = ref, pltpu.make_async_copy(ref, target, sem)

    def send(self):
        self.copy.start()

    def wait(self):
        self.copy.wait()


class Held:
    def __init__(self, array):
        self.array = array


class Load:
    def __init__(self, array):
        self.array = array


class HeldRef:
    def __init__(self, ref):
        self.ref = ref

    def get(self):
        return self.ref

    def send(self):
        pass

    def wait(self):
        pass


def call(kernel, outs, *args, scratch=()):
    given = [getattr(arg, "array", arg) for arg in args]
    loads = [arg.array for arg in args if isinstance(arg, Load)]
    made = [*[Held(load) for load in loads], *outs]
    plain = [arg for arg in args if not isinstance(arg, (Held, Load))]
    plain += [out for out in outs if not isinstance(out, Held)]

    def body(*refs):
        refs = list(refs)
        ins, refs = refs[: len(given)], refs[len(given) :]
        loaded, refs = refs[: len(loads)], refs[len(loads) :]
        results, refs = refs[: len(outs)], refs[len(outs) :]
        inner, refs = refs[: len(scratch)], refs[len(scratch) :]
        buffers, sems = refs[:-1], refs[-1]
        count = 0
        operands = []
        for arg, ref in zip(args, ins):
            if isinstance(arg, Held):
                operands.append(HeldRef(ref))
                continue
            target = loaded.pop(0) if isinstance(arg, Load) else buffers.pop(0)
            operands.append(Operand(ref, target, sems.at[count]))
            count += 1
        outputs = []
        for out, ref in zip(outs, results):
            if isinstance(out, Held):
                outputs.append(HeldRef(ref))
                continue
            outputs.append(Result(ref, buffers.pop(0), sems.at[count]))
            count += 1
        kernel(*operands, *outputs, *inner)
        for operand in operands:
            operand.get()
        for output in outputs:
            output.wait()

    def space(item):
        return pltpu.VMEM if isinstance(item, Held) else pltpu.HBM

    results = pl.pallas_call(
        body,
        out_shape=[space(m)(getattr(m, "array", m).shape, getattr(m, "array", m).dtype) for m in made],
        in_specs=[pl.BlockSpec(memory_space=space(arg)) for arg in args],
        out_specs=[pl.BlockSpec(memory_space=space(m)) for m in made],
        scratch_shapes=[
            *scratch,
            *[pltpu.VMEM(a.shape, a.dtype) for a in plain],
            pltpu.SemaphoreType.DMA((max(len(plain) + len(loads), 1),)),
        ],
        compiler_params=pltpu.CompilerParams(vmem_limit_bytes=24 * 2**20),
    )(*[pltpu.with_memory_space_constraint(a, space(arg)) for a, arg in zip(given, args)])
    return [Held(result) if isinstance(m, Held) else result for result, m in zip(results, made)]


def f32(*shape):
    return jax.ShapeDtypeStruct(shape, jnp.float32)


def b16(*shape):
    return jax.ShapeDtypeStruct(shape, jnp.bfloat16)


def held(shape):
    return Held(shape)


def bit_groups():
    frame_bits = lax.axis_size("frame").bit_length() - 1
    azim_bits = lax.axis_size("azim").bit_length() - 1
    frame = [1 << bit for bit in range(frame_bits)]
    azim = [1 << (bit + frame_bits) for bit in range(azim_bits)]
    return [frame[:1], azim[:1] + frame[1:2], azim[:0:-1] + frame[:1:-1]]


def exchange(block, mask):
    members = lax.axis_size(("azim", "frame"))
    return lax.ppermute(block, ("azim", "frame"), [(i, i ^ mask) for i in range(members)])


def row_order(channels):
    row = lax.broadcasted_iota(jnp.int32, (channels, channels), 0)
    column = lax.broadcasted_iota(jnp.int32, (channels, channels), 1)
    weights = sum(bit_groups(), [])
    members = 1 << len(weights)
    if channels % members == 0:
        each = channels // members
        me = lax.axis_index("azim") * lax.axis_size("frame") + lax.axis_index("frame")
        part = jnp.floor((row.astype(jnp.float32) + 0.5) * (1.0 / each)).astype(jnp.int32)
        row = row - part * each
        for stage, weight in enumerate(weights):
            far = (part >> (len(weights) - 1 - stage)) & 1
            own = (me >> (weight.bit_length() - 1)) & 1
            row = row + (far ^ own) * (weight * each)
    return jnp.where(column == row, 1.0, 0.0).astype(jnp.bfloat16)


def scatter_flat(terms):
    weights = sum(bit_groups(), [])
    members = 1 << len(weights)
    widths = [term.size // members for term in terms]
    held = jnp.concatenate([term.reshape(members, -1) for term in terms], 1).astype(jnp.bfloat16)
    held = held.reshape((2,) * len(weights) + (-1,))
    me = lax.axis_index(("azim", "frame"))
    for weight in weights:
        dim = len(weights) - weight.bit_length()
        own = (me >> (weight.bit_length() - 1)) & 1
        kept = lax.dynamic_slice_in_dim(held, own, 1, dim)
        got = exchange(lax.dynamic_slice_in_dim(held, 1 - own, 1, dim), weight)
        total = kept.astype(jnp.float32) + got.astype(jnp.float32)
        held = total.astype(jnp.bfloat16)
    total = total.reshape(-1)
    return total[: widths[0]], total[widths[0] :]


def swap(total, weights):
    count = 1 << len(weights)
    rows = total.shape[0] // count
    gots = []
    for block in range(count - 1, 0, -1):
        mask = sum(w for i, w in enumerate(weights) if block >> (len(weights) - 1 - i) & 1)
        part = total[block * rows : (block + 1) * rows].astype(jnp.bfloat16)
        gots.append(exchange(part, mask))
    return gots


def finish_kernel(split, total, *rest):
    gots, (attend_grad, output_grad) = rest[:-2], rest[-2:]
    rows = gots[0].ref.shape[0]
    sums = total.get()[:rows, :]
    for got in gots:
        sums = sums + got.get()[...].astype(jnp.float32)
    for out, first, last in ((attend_grad, 0, split), (output_grad, split, sums.shape[1])):
        tiles = (last - first) // LANES
        for tile in range(tiles):
            at = first + tile * LANES
            out.ref[pl.ds(tile, rows, stride=tiles), :] = sums[:, at : at + LANES]
        out.send()


def scatter_sum(kept, sent, channels):
    groups = bit_groups()
    split = 3 * channels
    if channels % (1 << len(sum(groups, []))):
        whole = jnp.concatenate([kept, sent.astype(jnp.float32)], 0)
        return scatter_flat((whole[:, :split], whole[:, split:]))
    total = kept + exchange(sent, groups[0][0]).astype(jnp.float32)
    gots = swap(total, groups[1])
    total = sum((got.astype(jnp.float32) for got in gots), total[: gots[0].shape[0]])
    gots = swap(total, groups[2])
    rows = gots[0].shape[0]
    attend_grad, output_grad = call(
        functools.partial(finish_kernel, split),
        (f32(rows * split // LANES, LANES), f32(rows * channels // LANES, LANES)),
        Held(total), *[Held(got) for got in gots],
    )
    return attend_grad.reshape(-1), output_grad.reshape(-1)


def from_behind(block, axis, distance):
    size = lax.axis_size(axis)
    return lax.ppermute(block, axis, [((i - distance) % size, i) for i in range(size)])


def per_device(features, position_bias, attend_weight, output_weight, merge_weight, cotangent):
    x, cot = features[0], cotangent[0]
    rows, cols, channels = x.shape
    heads = position_bias.shape[1]
    grid = Grid(rows, cols, heads, channels)
    width = cot.shape[2]
    bf16 = jnp.bfloat16
    halo_rows = grid.west_rows + width // channels * grid.cot_halo
    own, local, quads = grid.window_rows, grid.local_rows, 4 * grid.quad_count
    per_group = LANES * heads // channels
    groups, across = heads // per_group, per_group * SLOT
    lane_head = np.arange(LANES) // (channels // heads)
    head_mask = jnp.asarray(np.repeat(np.arange(per_group), SLOT)[:, None] == lane_head[None, :]).astype(bf16)
    (to_next,) = call(
        functools.partial(pre_kernel, grid), (held(b16(halo_rows, channels)),),
        x, cot, grid.pack_tokens(), grid.pack_cot(),
        scratch=[pltpu.VMEM((grid.own_rows, channels), bf16), pltpu.VMEM((grid.cot_own, width), bf16)],
    )
    from_west = Held(from_behind(to_next.array, "azim", 1))
    halo = grid.bands * SLOT
    (
        to_windows, attend_held, mask_held, merge_held, output_held, to_quads, cot_to_quads, from_quads, quads_back,
        tokens_back, final_tokens, final_quads, bias, mask, quad_tokens, windowed, normed_local, std_local,
        projected, attended, probs, orders, rolled_t, attended_t,
    ) = call(
        functools.partial(local_kernel, grid),
        (
            held(f32(groups, SLOT, across)), held(f32(SLOT, across)), held(b16(grid.cot_own, width)),
            held(f32(own, channels)), held(f32(local, channels)), held(f32(local, 1)),
            held(b16(local, 3 * channels)), held(b16(local, channels)),
            held(f32(grid.local_windows * groups, SLOT, across)),
            held(b16(channels, channels)),
            held(b16(channels, local)), held(b16(channels, local)),
        ),
        x, cot, position_bias.T, Load(grid.to_windows()), Load(attend_weight), Load(head_mask), Load(merge_weight),
        Load(output_weight), Load(grid.to_quads()), Load(grid.cot_to_quads()), Load(grid.from_quads()),
        Load(grid.quads_back()), Load(grid.tokens_back()), Load(grid.final_tokens()), Load(grid.final_quads()),
        scratch=[pltpu.VMEM((grid.own_rows, channels), bf16)],
    )
    half = channels // 2
    kept, sent, projected_grad, normed, inverse_std, branch_grad, quad16 = call(
        functools.partial(main_kernel, grid),
        (
            held(f32(half, 4 * channels)), held(b16(half, 4 * channels)), held(b16(own, 3 * channels)),
            held(f32(own, channels)), held(f32(own, 1)), held(b16(own, channels)), held(b16(quads, channels)),
        ),
        from_west, to_windows, attend_held, mask_held, bias, mask, to_quads, output_held, cot_to_quads, merge_held,
        from_quads, quad_tokens, windowed, normed_local, std_local, projected, attended, probs, orders,
        rolled_t, attended_t,
        scratch=[
            pltpu.VMEM((halo, 3 * channels), bf16),
            pltpu.VMEM((halo, channels), bf16),
            pltpu.VMEM((grid.bands * groups, SLOT, across), jnp.float32),
            pltpu.VMEM((own, channels), bf16),
            pltpu.VMEM((4, grid.quad_count, channels), jnp.float32),
            pltpu.VMEM((channels, halo), bf16),
            pltpu.VMEM((channels, halo), bf16),
        ],
    )
    (merged_quads,) = call(
        functools.partial(merge_kernel, grid), (held(b16(grid.quad_count, width)),), quad16, merge_held
    )
    back, feature_grads = call(
        functools.partial(tail_kernel, grid), (held(b16(halo_rows, channels)), held(b16(own, channels))),
        projected_grad, attend_held, normed, inverse_std, branch_grad, quads_back, tokens_back, merged_quads,
    )
    came = Held(from_behind(back.array, "azim", -1))
    feature_grad, merged = call(
        functools.partial(last_kernel, grid),
        (b16(rows, cols, channels), b16(grid.quad_lines, grid.quad_cols, width)),
        feature_grads, merged_quads, came, final_tokens, final_quads,
    )
    attend_grad, output_grad = scatter_sum(kept.array, sent.array, channels)
    return (merged[None], feature_grad[None], attend_grad, output_grad)


def solution(mesh):
    in_specs = (P("frame", None, "azim", None), P(), P(), P(), P(), P("frame", None, "azim", None))
    out_specs = (
        P("frame", None, "azim", None),
        P("frame", None, "azim", None),
        P(("azim", "frame")),
        P(("azim", "frame")),
    )

    return jax.shard_map(per_device, mesh=mesh, in_specs=in_specs, out_specs=out_specs, check_vma=False)
```

```python
import functools

import jax
import jax.numpy as jnp
import numpy as np
from jax import lax
from jax.experimental import pallas as pl
from jax.experimental.pallas import tpu as pltpu
from jax.sharding import PartitionSpec as P


WINDOW = 7
SHIFT = 3
SLOT = 64
LANES = 128
EPS = 1e-05


def up(value, step):
    return -(-value // step) * step


def dot(left, right):
    return lax.dot_general(left, right, (((1,), (0,)), ((), ())), preferred_element_type=jnp.float32)


def dot_t(left, right):
    return lax.dot_general(left, right, (((1,), (1,)), ((), ())), preferred_element_type=jnp.float32)


def pick(select, values):
    return dot(select, values).astype(jnp.bfloat16)


class Grid:
    def __init__(self, rows, cols, heads, channels):
        self.rows, self.cols, self.heads, self.channels = rows, cols, heads, channels
        self.west = WINDOW - SHIFT
        self.last = cols - self.west
        self.bands, self.across = rows // WINDOW, cols // WINDOW
        self.windows = self.bands * self.across
        self.local_windows = self.windows - self.bands
        self.window_rows, self.local_rows = self.windows * SLOT, self.local_windows * SLOT
        self.stride = up(cols, 16)
        self.own_rows = rows * self.stride
        self.west_rows = up(rows * self.west, 16)
        self.quad_lines, self.quad_cols, self.quad_west = rows // 2, cols // 2, self.west // 2
        self.quad_stride = up(self.quad_cols, 8)
        self.quad_count = up(self.quad_lines * self.quad_stride, 16)
        self.cot_stride = up(self.quad_cols, 16)
        self.cot_own = self.quad_lines * self.cot_stride
        self.cot_halo = up(self.quad_west * self.quad_lines, 16)

    def source(self, row, col):
        return row * self.stride + col if col >= 0 else self.own_rows + row * self.west + col + self.west

    def window_row(self, row, col):
        line = (row - SHIFT) % self.rows
        across, place = divmod(col + self.west, WINDOW)
        window = (across - 1) % self.across * self.bands + line // WINDOW
        return window * SLOT + line % WINDOW * (WINDOW + 1) + place

    def quad_row(self, row, col):
        phase = 2 * (col % 2) + row % 2
        return phase * self.quad_count + row // 2 * self.quad_stride + (col + self.west) // 2

    def onehot(self, shape, pairs):
        out = np.zeros(shape, np.float32)
        for i, j in pairs:
            out[i, j] = 1
        return jnp.asarray(out, jnp.bfloat16)

    def cells(self, first, last):
        return [(r, c) for r in range(self.rows) for c in range(first, last)]

    def to_windows(self):
        pairs = [(self.window_row(r, c), self.source(r, c)) for r, c in self.cells(-self.west, self.last)]
        return self.onehot((self.window_rows, self.own_rows + self.west_rows), pairs)

    def to_quads(self):
        pairs = [(self.quad_row(r, c), self.window_row(r, c)) for r, c in self.cells(-self.west, self.last)]
        return self.onehot((4 * self.quad_count, self.window_rows), pairs)

    def from_quads(self):
        return self.to_quads().T

    def pack_tokens(self):
        pairs = [
            (r * self.west + c - self.last, self.source(r, c)) for r, c in self.cells(self.last, self.cols)
        ]
        return self.onehot((self.west_rows, self.own_rows), pairs)

    def quad_cells(self, first, last):
        return [(i, j) for i in range(self.quad_lines) for j in range(first, last)]

    def pack_cot(self):
        first = self.quad_cols - self.quad_west
        pairs = [
            (self.quad_west * i + j - first, i * self.cot_stride + j)
            for i, j in self.quad_cells(first, self.quad_cols)
        ]
        return self.onehot((self.cot_halo, self.cot_own), pairs)

    def cot_to_quads(self):
        pairs = [
            (i * self.quad_stride + j, self.cot_own + self.quad_west * i + j)
            for i, j in self.quad_cells(0, self.quad_west)
        ]
        pairs += [
            (i * self.quad_stride + j, i * self.cot_stride + j - self.quad_west)
            for i, j in self.quad_cells(self.quad_west, self.quad_cols)
        ]
        return self.onehot((self.quad_count, self.cot_own + self.cot_halo), pairs)

    def tokens_back(self):
        pairs = [(r * self.west + c + self.west, self.window_row(r, c)) for r, c in self.cells(-self.west, 0)]
        return self.onehot((self.west_rows, self.window_rows), pairs)

    def quads_back(self):
        pairs = [
            (self.quad_west * i + j, i * self.quad_stride + j) for i, j in self.quad_cells(0, self.quad_west)
        ]
        return self.onehot((self.cot_halo, self.quad_count), pairs)

    def final_tokens(self):
        pairs = [(self.source(r, c), self.window_row(r, c)) for r, c in self.cells(0, self.last)]
        pairs += [
            (self.source(r, c), self.window_rows + r * self.west + c - self.last)
            for r, c in self.cells(self.last, self.cols)
        ]
        return self.onehot((self.own_rows, self.window_rows + self.west_rows), pairs)

    def final_quads(self):
        first = self.quad_cols - self.quad_west
        pairs = [
            (i * self.quad_stride + j, i * self.quad_stride + j + self.quad_west)
            for i, j in self.quad_cells(0, first)
        ]
        pairs += [
            (i * self.quad_stride + j, self.quad_count + self.quad_west * i + j - first)
            for i, j in self.quad_cells(first, self.quad_cols)
        ]
        return self.onehot((self.quad_count, self.quad_count + self.cot_halo), pairs)


def normalize(values):
    centred = values - jnp.mean(values, -1, keepdims=True)
    inverse_std = lax.rsqrt(jnp.mean(centred * centred, -1, keepdims=True) + EPS)
    return centred * inverse_std, inverse_std


def spread(ref, grid_ref, stride):
    ref[0 : grid_ref.shape[0] * stride, :] = jnp.zeros((grid_ref.shape[0] * stride, ref.shape[1]), ref.dtype)
    for line in range(grid_ref.shape[0]):
        ref[line * stride : line * stride + grid_ref.shape[1], :] = grid_ref[line]


def pack(grid, out, tokens, quads):
    out[0 : grid.west_rows, :] = tokens
    for part in range(quads.shape[1] // grid.channels):
        first = grid.west_rows + part * grid.cot_halo
        out[first : first + grid.cot_halo, :] = quads[:, part * grid.channels : (part + 1) * grid.channels]


def unpack(grid, ref, width):
    first = grid.west_rows
    parts = [
        ref[first + part * grid.cot_halo : first + (part + 1) * grid.cot_halo, :]
        for part in range(width // grid.channels)
    ]
    return ref[0 : grid.west_rows, :], jnp.concatenate(parts, 1)


def pre_kernel(grid, x, cot, pack_tokens, pack_cot, to_next, tokens, quads):
    spread(tokens, x.get(), grid.stride)
    spread(quads, cot.get(), grid.cot_stride)
    halo = pick(pack_cot.get()[...], quads[...])
    pack(grid, to_next.ref, pick(pack_tokens.get()[...], tokens[...]), halo)
    to_next.send()


def build_bias(grid, table, bias, mask):
    span, count = 2 * WINDOW - 1, WINDOW + 1
    per_group = LANES * grid.heads // grid.channels
    center = (WINDOW - 1) * span + WINDOW - 1
    rows = table.shape[1]
    values = jnp.concatenate([table[...], jnp.zeros((table.shape[0], 2 * LANES - rows), jnp.float32)], 1)
    key = lax.broadcasted_iota(jnp.int32, (SLOT, per_group * SLOT), 0)
    query = lax.broadcasted_iota(jnp.int32, (SLOT, per_group * SLOT), 1) & (SLOT - 1)
    key_row, key_col = key >> 3, key & (count - 1)
    query_row = query >> 3
    padded = jnp.where((key_row < WINDOW) & (key_col < WINDOW), 0.0, -1e30)
    key_late = (key_row >= WINDOW - SHIFT).astype(jnp.int32)
    query_late = (query_row >= WINDOW - SHIFT).astype(jnp.int32)
    mask[...] = jnp.where(key_late != query_late, -100.0, 0.0)
    place = lax.broadcasted_iota(jnp.int32, (LANES, per_group * SLOT), 0)
    lane = lax.broadcasted_iota(jnp.int32, (LANES, per_group * SLOT), 1)
    inside = lane & (SLOT - 1)
    wanted = (inside >> 3) * span + (inside & (count - 1))
    hit = (place == wanted) & ((inside >> 3) < WINDOW) & ((inside & (count - 1)) < WINDOW)
    for group in range(grid.heads // per_group):
        total = padded
        for head in range(per_group):
            line = jnp.broadcast_to(values[group * per_group + head : group * per_group + head + 1], (count, 2 * LANES))
            line = pltpu.roll(line, 0, 1, stride=1, stride_axis=0)
            blocks = [
                pltpu.roll(line, (span * r - center) % (2 * LANES), 1)[:, :LANES] for r in range(WINDOW)
            ]
            blocks.append(jnp.zeros((count, LANES), jnp.float32))
            block = jnp.concatenate(blocks, 0)
            high = block.astype(jnp.bfloat16)
            low = (block - high.astype(jnp.float32)).astype(jnp.bfloat16)
            select = jnp.where(hit & ((lane // SLOT) == head), 1.0, 0.0).astype(jnp.bfloat16)
            total = total + dot(high, select) + dot(low, select)
        bias[group] = total


class Heads:
    def __init__(self, grid, head_mask):
        self.channels = grid.channels
        self.head_size = grid.channels // grid.heads
        self.scale = self.head_size ** (-0.5)
        self.per_group = LANES // self.head_size
        self.groups = grid.heads // self.per_group
        self.head_mask = head_mask

    def spread(self, values):
        return jnp.concatenate([values] * self.per_group, 0) * self.head_mask

    def collect(self, stacked):
        total = None
        for head in range(self.per_group):
            part = stacked[head * SLOT : (head + 1) * SLOT, :]
            part = jnp.where(self.head_mask[head * SLOT : (head + 1) * SLOT, :] > 0, part, 0.0)
            total = part if total is None else total + part
        return total

    def split(self, projected, window, group):
        rows = slice(window * SLOT, (window + 1) * SLOT)
        firsts = [part * self.channels + group * LANES for part in range(3)]
        return [projected[rows, first : first + LANES] for first in firsts]

    def forward(self, jobs, fillers=()):
        def product(job):
            query, key, value = self.split(job.projected, job.window, job.group)
            return dot_t(key, self.spread(query)), value

        def soften(job, scores, value):
            scores = scores * self.scale + job.bias[job.group]
            if job.extra is not None:
                scores = scores + job.extra[...]
            weights = jnp.exp(scores - jnp.max(scores, 0, keepdims=True))
            prob = weights / jnp.sum(weights, 0, keepdims=True)
            job.probs[job.window * self.groups + job.group] = prob
            return prob.astype(jnp.bfloat16), value

        def mix(job, prob, value):
            return (dot(prob.T, value),)

        def store(job, mixed):
            rows, lanes = job.window * SLOT, job.group * LANES
            job.attended[rows : rows + SLOT, lanes : lanes + LANES] = self.collect(mixed).astype(jnp.bfloat16)
            return ()

        interleave(jobs, (product, soften, mix, store), fillers)

    def backward(self, jobs, outer, projected_grad, fillers=()):
        def rows_of(job):
            return slice(job.first + job.window * SLOT, job.first + (job.window + 1) * SLOT)

        def put(job, part, grad):
            at = part * self.channels + job.group * LANES
            projected_grad[rows_of(job), at : at + LANES] = grad.astype(jnp.bfloat16)

        def product(job):
            value = self.split(job.projected, job.window, job.group)[2]
            grads = self.spread(outer[rows_of(job), job.group * LANES : (job.group + 1) * LANES])
            prob = job.probs[job.window * self.groups + job.group]
            put(job, 2, dot(prob.astype(jnp.bfloat16), grads))
            return (dot_t(value, grads),)

        def soften(job, score_grad):
            prob = job.probs[job.window * self.groups + job.group]
            inner = jnp.sum(prob * score_grad, 0, keepdims=True)
            return ((prob * (score_grad - inner) * self.scale).astype(jnp.bfloat16),)

        def mix(job, soft):
            query, key, _ = self.split(job.projected, job.window, job.group)
            put(job, 1, dot(soft, self.spread(query)))
            return (dot(soft.T, key),)

        def store(job, mixed):
            put(job, 0, self.collect(mixed))
            return ()

        interleave(jobs, (product, soften, mix, store), fillers)


class Job:
    def __init__(self, **fields):
        self.__dict__.update(fields)


def jobs_of(windows, groups, **fields):
    return [Job(window=window, group=group, **fields) for window in range(windows) for group in range(groups)]


def interleave(jobs, stages, fillers=()):
    states = [()] * len(jobs)
    fillers = list(fillers)
    for turn in range(len(jobs) + len(stages) - 1):
        for depth, stage in reversed(list(enumerate(stages))):
            at = turn - depth
            if 0 <= at < len(jobs):
                states[at] = stage(jobs[at], *states[at])
        if fillers:
            fillers.pop(0)()
    for filler in fillers:
        filler()


def with_masks(jobs, grid, mask):
    for job in jobs:
        job.extra = mask if job.window % grid.bands == grid.bands - 1 else None
    return jobs


def local_kernel(grid, x, cot, table, to_windows, attend_weight, head_mask, *rest):
    tokens = rest[-1]
    bias, mask, quads, windowed, normed, std, projected, attended, probs, orders, rolled_t, attended_t = [
        r.ref for r in rest[-13:-1]
    ]
    spread(quads, cot.get(), grid.cot_stride)
    spread(tokens, x.get(), grid.stride)
    build_bias(grid, table.get(), bias, mask)
    values = dot(to_windows.get()[:, : grid.own_rows], tokens[...])
    windowed[...] = values
    local = grid.local_rows
    n, inverse_std = normalize(values[:local])
    normed[...] = n
    std[...] = inverse_std
    projected[...] = dot(n.astype(jnp.bfloat16), attend_weight.get()[...]).astype(jnp.bfloat16)
    heads = Heads(grid, head_mask.get()[...])
    jobs = jobs_of(
        grid.local_windows, heads.groups, projected=projected, bias=bias, attended=attended, probs=probs
    )
    heads.forward(with_masks(jobs, grid, mask))
    rolled = n.astype(jnp.bfloat16)
    order = row_order(grid.channels)
    orders[...] = order
    rolled_t[...] = dot_t(order, rolled).astype(jnp.bfloat16)
    attended_t[...] = dot_t(order, attended[...]).astype(jnp.bfloat16)


def main_kernel(
    grid, from_west, to_windows, attend_weight, head_mask, bias, mask, to_quads, output_weight,
    cot_to_quads, merge_weight, from_quads, quads, windowed_own, normed_local, std_local, projected_local,
    attended_local, probs_local, orders, rolled_t_local, attended_t_local,
    kept, sent, projected_grad_out, normed_out, std_out, branch_grad_out, quad16_out,
    projected, attended, probs, outer, quad_grads, rolled_t, attended_t,
):
    channels, local = grid.channels, grid.local_rows
    west_tokens, west_quads = unpack(grid, from_west.get(), quads.ref.shape[1])
    windowed = windowed_own.ref[...] + dot(to_windows.ref[:, grid.own_rows :], west_tokens)
    normed, inverse_std = normalize(windowed[local:])
    normed_out.ref[:local] = normed_local.ref[...]
    normed_out.ref[local:] = normed
    std_out.ref[:local] = std_local.ref[...]
    std_out.ref[local:] = inverse_std
    projected[...] = dot(normed.astype(jnp.bfloat16), attend_weight.ref[...]).astype(jnp.bfloat16)
    rolled = normed.astype(jnp.bfloat16)
    cot_select = cot_to_quads.ref
    cot_quads = dot(cot_select[:, : grid.cot_own], quads.ref[: grid.cot_own, :])
    cot_quads = (cot_quads + dot(cot_select[:, grid.cot_own :], west_quads)).astype(jnp.bfloat16)
    merge_ref = merge_weight.ref

    def quad_product(k):
        quad_grads[k] = dot_t(cot_quads, merge_ref[k * channels : (k + 1) * channels, :])

    heads = Heads(grid, head_mask.ref[...])
    jobs = jobs_of(grid.bands, heads.groups, projected=projected, bias=bias.ref, attended=attended, probs=probs)
    heads.forward(
        with_masks(jobs, grid, mask.ref), [functools.partial(quad_product, k) for k in range(4)]
    )

    select = to_quads.ref
    attended_quads = (
        dot(select[:, :local], attended_local.ref[...]) + dot(select[:, local:], attended[...])
    ).astype(jnp.bfloat16)
    feature_quads = dot(select[...], windowed.astype(jnp.bfloat16))
    branch = dot(attended_quads, output_weight.ref[...])
    hidden = (feature_quads + branch).astype(jnp.bfloat16).astype(jnp.float32)
    count = grid.quad_count
    phases = [hidden[k * count : (k + 1) * count] for k in range(4)]
    width = 4 * channels
    mean = sum(jnp.sum(phase, -1, keepdims=True) for phase in phases) / width
    centred = [phase - mean for phase in phases]
    variance = sum(jnp.sum(phase * phase, -1, keepdims=True) for phase in centred) / width
    quad_std = lax.rsqrt(variance + EPS)
    quad_normed = [phase * quad_std for phase in centred]
    for k in range(4):
        quad16_out.ref[k * count : (k + 1) * count, :] = quad_normed[k].astype(jnp.bfloat16)
    first = sum(jnp.sum(quad_grads[k], -1, keepdims=True) for k in range(4)) / width
    second = sum(jnp.sum(quad_grads[k] * quad_normed[k], -1, keepdims=True) for k in range(4)) / width
    hidden_grad = jnp.concatenate(
        [quad_std * (quad_grads[k] - first - quad_normed[k] * second) for k in range(4)], 0
    ).astype(jnp.bfloat16)
    branch_grad = pick(from_quads.ref[...], hidden_grad)
    branch_grad_out.ref[...] = branch_grad
    outer[...] = dot_t(branch_grad, output_weight.ref[...]).astype(jnp.bfloat16)
    projected_grad = projected_grad_out.ref
    jobs = jobs_of(
        grid.local_windows, heads.groups, projected=projected_local.ref, probs=probs_local.ref, first=0
    )
    jobs += jobs_of(grid.bands, heads.groups, projected=projected, probs=probs, first=local)

    def turned():
        rolled_t[...] = dot_t(orders.ref[...], rolled).astype(jnp.bfloat16)

    def turned_attended():
        attended_t[...] = dot_t(orders.ref[...], attended[...]).astype(jnp.bfloat16)

    heads.backward(jobs, outer, projected_grad, [turned_attended, turned])

    half, joint = channels // 2, 3 * channels

    def put(first, local_t, halo_t, grads):
        piece = dot(local_t, grads[:local]) + dot(halo_t, grads[local:])
        kept.ref[:, first : first + piece.shape[1]] = piece[:half]
        sent.ref[:, first : first + piece.shape[1]] = piece[half:].astype(jnp.bfloat16)

    put(joint, attended_t_local.ref[...], attended_t[...], branch_grad)
    for first in range(0, joint, channels):
        put(first, rolled_t_local.ref[...], rolled_t[...], projected_grad[:, first : first + channels])


def tail_kernel(
    grid, projected_grad, attend_weight, normed, inverse_std, branch_grad, quads_back, tokens_back, merged,
    back, feature_grads,
):
    grads = dot_t(projected_grad.get()[...], attend_weight.get()[...])
    n = normed.get()[...]
    first = jnp.mean(grads, -1, keepdims=True)
    second = jnp.mean(grads * n, -1, keepdims=True)
    rolled_grad = inverse_std.get()[...] * (grads - first - n * second)
    total = (branch_grad.get()[...].astype(jnp.float32) + rolled_grad).astype(jnp.bfloat16)
    feature_grads.ref[...] = total
    feature_grads.send()
    pack(grid, back.ref, pick(tokens_back.get()[...], total), pick(quads_back.get()[...], merged.get()[...]))
    back.send()


def merge_kernel(grid, quad16, merge_weight, merged):
    channels, count = grid.channels, grid.quad_count
    sums = None
    quad_ref, merge_ref = quad16.get(), merge_weight.get()
    for k in range(4):
        term = dot(quad_ref[k * count : (k + 1) * count, :], merge_ref[k * channels : (k + 1) * channels, :])
        sums = term if sums is None else sums + term
    merged.ref[...] = sums.astype(jnp.bfloat16)
    merged.send()


def last_kernel(grid, feature_grads, merged, came, final_tokens, final_quads, out, merged_out):
    width = merged_out.ref.shape[2]
    tokens, quads = unpack(grid, came.get(), width)
    rows = grid.window_rows
    select = final_tokens.get()
    total = dot(select[:, :rows], feature_grads.get()[...]) + dot(select[:, rows:], tokens)
    for line in range(grid.rows):
        out.ref[line] = total[line * grid.stride : line * grid.stride + grid.cols].astype(jnp.bfloat16)
    out.send()
    select = final_quads.get()
    count = grid.quad_count
    sums = dot(select[:, :count], merged.get()[...]) + dot(select[:, count:], quads)
    for line in range(grid.quad_lines):
        first = line * grid.quad_stride
        merged_out.ref[line] = sums[first : first + grid.quad_cols].astype(jnp.bfloat16)
    merged_out.send()


class Operand:
    def __init__(self, source, ref, sem):
        self.ref, self.copy, self.waited = ref, pltpu.make_async_copy(source, ref, sem), False
        self.copy.start()

    def get(self):
        if not self.waited:
            self.copy.wait()
            self.waited = True
        return self.ref


class Result:
    def __init__(self, target, ref, sem):
        self.ref, self.copy = ref, pltpu.make_async_copy(ref, target, sem)

    def send(self):
        self.copy.start()

    def wait(self):
        self.copy.wait()


class Held:
    def __init__(self, array):
        self.array = array


class Load:
    def __init__(self, array):
        self.array = array


class HeldRef:
    def __init__(self, ref):
        self.ref = ref

    def get(self):
        return self.ref

    def send(self):
        pass

    def wait(self):
        pass


def call(kernel, outs, *args, scratch=()):
    given = [getattr(arg, "array", arg) for arg in args]
    loads = [arg.array for arg in args if isinstance(arg, Load)]
    made = [*[Held(load) for load in loads], *outs]
    plain = [arg for arg in args if not isinstance(arg, (Held, Load))]
    plain += [out for out in outs if not isinstance(out, Held)]

    def body(*refs):
        refs = list(refs)
        ins, refs = refs[: len(given)], refs[len(given) :]
        loaded, refs = refs[: len(loads)], refs[len(loads) :]
        results, refs = refs[: len(outs)], refs[len(outs) :]
        inner, refs = refs[: len(scratch)], refs[len(scratch) :]
        buffers, sems = refs[:-1], refs[-1]
        count = 0
        operands = []
        for arg, ref in zip(args, ins):
            if isinstance(arg, Held):
                operands.append(HeldRef(ref))
                continue
            target = loaded.pop(0) if isinstance(arg, Load) else buffers.pop(0)
            operands.append(Operand(ref, target, sems.at[count]))
            count += 1
        outputs = []
        for out, ref in zip(outs, results):
            if isinstance(out, Held):
                outputs.append(HeldRef(ref))
                continue
            outputs.append(Result(ref, buffers.pop(0), sems.at[count]))
            count += 1
        kernel(*operands, *outputs, *inner)
        for operand in operands:
            operand.get()
        for output in outputs:
            output.wait()

    def space(item):
        return pltpu.VMEM if isinstance(item, Held) else pltpu.HBM

    results = pl.pallas_call(
        body,
        out_shape=[space(m)(getattr(m, "array", m).shape, getattr(m, "array", m).dtype) for m in made],
        in_specs=[pl.BlockSpec(memory_space=space(arg)) for arg in args],
        out_specs=[pl.BlockSpec(memory_space=space(m)) for m in made],
        scratch_shapes=[
            *scratch,
            *[pltpu.VMEM(a.shape, a.dtype) for a in plain],
            pltpu.SemaphoreType.DMA((max(len(plain) + len(loads), 1),)),
        ],
        compiler_params=pltpu.CompilerParams(vmem_limit_bytes=24 * 2**20),
    )(*[pltpu.with_memory_space_constraint(a, space(arg)) for a, arg in zip(given, args)])
    return [Held(result) if isinstance(m, Held) else result for result, m in zip(results, made)]


def f32(*shape):
    return jax.ShapeDtypeStruct(shape, jnp.float32)


def b16(*shape):
    return jax.ShapeDtypeStruct(shape, jnp.bfloat16)


def held(shape):
    return Held(shape)


def bit_groups():
    frame_bits = lax.axis_size("frame").bit_length() - 1
    azim_bits = lax.axis_size("azim").bit_length() - 1
    frame = [1 << bit for bit in range(frame_bits)]
    azim = [1 << (bit + frame_bits) for bit in range(azim_bits)]
    return [frame[:1], azim[:1] + frame[1:2], azim[:0:-1] + frame[:1:-1]]


def exchange(block, mask):
    members = lax.axis_size(("azim", "frame"))
    return lax.ppermute(block, ("azim", "frame"), [(i, i ^ mask) for i in range(members)])


def row_order(channels):
    row = lax.broadcasted_iota(jnp.int32, (channels, channels), 0)
    column = lax.broadcasted_iota(jnp.int32, (channels, channels), 1)
    weights = sum(bit_groups(), [])
    members = 1 << len(weights)
    if channels % members == 0:
        each = channels // members
        me = lax.axis_index("azim") * lax.axis_size("frame") + lax.axis_index("frame")
        part = jnp.floor((row.astype(jnp.float32) + 0.5) * (1.0 / each)).astype(jnp.int32)
        row = row - part * each
        for stage, weight in enumerate(weights):
            far = (part >> (len(weights) - 1 - stage)) & 1
            own = (me >> (weight.bit_length() - 1)) & 1
            row = row + (far ^ own) * (weight * each)
    return jnp.where(column == row, 1.0, 0.0).astype(jnp.bfloat16)


def scatter_flat(terms):
    weights = sum(bit_groups(), [])
    members = 1 << len(weights)
    widths = [term.size // members for term in terms]
    held = jnp.concatenate([term.reshape(members, -1) for term in terms], 1).astype(jnp.bfloat16)
    held = held.reshape((2,) * len(weights) + (-1,))
    me = lax.axis_index(("azim", "frame"))
    for weight in weights:
        dim = len(weights) - weight.bit_length()
        own = (me >> (weight.bit_length() - 1)) & 1
        kept = lax.dynamic_slice_in_dim(held, own, 1, dim)
        got = exchange(lax.dynamic_slice_in_dim(held, 1 - own, 1, dim), weight)
        total = kept.astype(jnp.float32) + got.astype(jnp.float32)
        held = total.astype(jnp.bfloat16)
    total = total.reshape(-1)
    return total[: widths[0]], total[widths[0] :]


def swap(total, weights, blocks):
    count = 1 << len(weights)
    rows = total.shape[0] // count
    gots = []
    for block in blocks:
        mask = sum(w for i, w in enumerate(weights) if block >> (len(weights) - 1 - i) & 1)
        part = total[block * rows : (block + 1) * rows].astype(jnp.bfloat16)
        gots.append(exchange(part, mask))
    return gots


def finish_kernel(split, total, *rest):
    gots, (attend_grad, output_grad) = rest[:-2], rest[-2:]
    rows = gots[0].ref.shape[0]
    sums = total.get()[:rows, :]
    for got in gots:
        sums = sums + got.get()[...].astype(jnp.float32)
    for out, first, last in ((attend_grad, 0, split), (output_grad, split, sums.shape[1])):
        tiles = (last - first) // LANES
        for tile in range(tiles):
            at = first + tile * LANES
            out.ref[pl.ds(tile, rows, stride=tiles), :] = sums[:, at : at + LANES]
        out.send()


def scatter_sum(kept, sent, channels):
    groups = bit_groups()
    split = 3 * channels
    if channels % (1 << len(sum(groups, []))):
        whole = jnp.concatenate([kept, sent.astype(jnp.float32)], 0)
        return scatter_flat((whole[:, :split], whole[:, split:]))
    total = kept + exchange(sent, groups[0][0]).astype(jnp.float32)
    gots = swap(total, groups[1], (3, 2, 1))
    total = sum((got.astype(jnp.float32) for got in gots), total[: gots[0].shape[0]])
    gots = swap(total, groups[2], (2, 1, 3))
    rows = gots[0].shape[0]
    attend_grad, output_grad = call(
        functools.partial(finish_kernel, split),
        (f32(rows * split // LANES, LANES), f32(rows * channels // LANES, LANES)),
        Held(total), *[Held(got) for got in gots],
    )
    return attend_grad.reshape(-1), output_grad.reshape(-1)


def from_behind(block, axis, distance):
    size = lax.axis_size(axis)
    return lax.ppermute(block, axis, [((i - distance) % size, i) for i in range(size)])


def per_device(features, position_bias, attend_weight, output_weight, merge_weight, cotangent):
    x, cot = features[0], cotangent[0]
    rows, cols, channels = x.shape
    heads = position_bias.shape[1]
    grid = Grid(rows, cols, heads, channels)
    width = cot.shape[2]
    bf16 = jnp.bfloat16
    halo_rows = grid.west_rows + width // channels * grid.cot_halo
    own, local, quads = grid.window_rows, grid.local_rows, 4 * grid.quad_count
    per_group = LANES * heads // channels
    groups, across = heads // per_group, per_group * SLOT
    lane_head = np.arange(LANES) // (channels // heads)
    head_mask = jnp.asarray(np.repeat(np.arange(per_group), SLOT)[:, None] == lane_head[None, :]).astype(bf16)
    (to_next,) = call(
        functools.partial(pre_kernel, grid), (held(b16(halo_rows, channels)),),
        x, cot, grid.pack_tokens(), grid.pack_cot(),
        scratch=[pltpu.VMEM((grid.own_rows, channels), bf16), pltpu.VMEM((grid.cot_own, width), bf16)],
    )
    from_west = Held(from_behind(to_next.array, "azim", 1))
    halo = grid.bands * SLOT
    (
        to_windows, attend_held, mask_held, merge_held, output_held, to_quads, cot_to_quads, from_quads, quads_back,
        tokens_back, final_tokens, final_quads, bias, mask, quad_tokens, windowed, normed_local, std_local,
        projected, attended, probs, orders, rolled_t, attended_t,
    ) = call(
        functools.partial(local_kernel, grid),
        (
            held(f32(groups, SLOT, across)), held(f32(SLOT, across)), held(b16(grid.cot_own, width)),
            held(f32(own, channels)), held(f32(local, channels)), held(f32(local, 1)),
            held(b16(local, 3 * channels)), held(b16(local, channels)),
            held(f32(grid.local_windows * groups, SLOT, across)),
            held(b16(channels, channels)),
            held(b16(channels, local)), held(b16(channels, local)),
        ),
        x, cot, position_bias.T, Load(grid.to_windows()), Load(attend_weight), Load(head_mask), Load(merge_weight),
        Load(output_weight), Load(grid.to_quads()), Load(grid.cot_to_quads()), Load(grid.from_quads()),
        Load(grid.quads_back()), Load(grid.tokens_back()), Load(grid.final_tokens()), Load(grid.final_quads()),
        scratch=[pltpu.VMEM((grid.own_rows, channels), bf16)],
    )
    half = channels // 2
    kept, sent, projected_grad, normed, inverse_std, branch_grad, quad16 = call(
        functools.partial(main_kernel, grid),
        (
            held(f32(half, 4 * channels)), held(b16(half, 4 * channels)), held(b16(own, 3 * channels)),
            held(f32(own, channels)), held(f32(own, 1)), held(b16(own, channels)), held(b16(quads, channels)),
        ),
        from_west, to_windows, attend_held, mask_held, bias, mask, to_quads, output_held, cot_to_quads, merge_held,
        from_quads, quad_tokens, windowed, normed_local, std_local, projected, attended, probs, orders,
        rolled_t, attended_t,
        scratch=[
            pltpu.VMEM((halo, 3 * channels), bf16),
            pltpu.VMEM((halo, channels), bf16),
            pltpu.VMEM((grid.bands * groups, SLOT, across), jnp.float32),
            pltpu.VMEM((own, channels), bf16),
            pltpu.VMEM((4, grid.quad_count, channels), jnp.float32),
            pltpu.VMEM((channels, halo), bf16),
            pltpu.VMEM((channels, halo), bf16),
        ],
    )
    (merged_quads,) = call(
        functools.partial(merge_kernel, grid), (held(b16(grid.quad_count, width)),), quad16, merge_held
    )
    back, feature_grads = call(
        functools.partial(tail_kernel, grid), (held(b16(halo_rows, channels)), held(b16(own, channels))),
        projected_grad, attend_held, normed, inverse_std, branch_grad, quads_back, tokens_back, merged_quads,
    )
    came = Held(from_behind(back.array, "azim", -1))
    feature_grad, merged = call(
        functools.partial(last_kernel, grid),
        (b16(rows, cols, channels), b16(grid.quad_lines, grid.quad_cols, width)),
        feature_grads, merged_quads, came, final_tokens, final_quads,
    )
    attend_grad, output_grad = scatter_sum(kept.array, sent.array, channels)
    return (merged[None], feature_grad[None], attend_grad, output_grad)


def solution(mesh):
    in_specs = (P("frame", None, "azim", None), P(), P(), P(), P(), P("frame", None, "azim", None))
    out_specs = (
        P("frame", None, "azim", None),
        P("frame", None, "azim", None),
        P(("azim", "frame")),
        P(("azim", "frame")),
    )

    return jax.shard_map(per_device, mesh=mesh, in_specs=in_specs, out_specs=out_specs, check_vma=False)
```

```python
import functools

import jax
import jax.numpy as jnp
import numpy as np
from jax import lax
from jax.experimental import pallas as pl
from jax.experimental.pallas import tpu as pltpu
from jax.sharding import PartitionSpec as P


WINDOW = 7
SHIFT = 3
SLOT = 64
LANES = 128
EPS = 1e-05


def up(value, step):
    return -(-value // step) * step


def dot(left, right):
    return lax.dot_general(left, right, (((1,), (0,)), ((), ())), preferred_element_type=jnp.float32)


def dot_t(left, right):
    return lax.dot_general(left, right, (((1,), (1,)), ((), ())), preferred_element_type=jnp.float32)


def pick(select, values):
    return dot(select, values).astype(jnp.bfloat16)


class Grid:
    def __init__(self, rows, cols, heads, channels):
        self.rows, self.cols, self.heads, self.channels = rows, cols, heads, channels
        self.west = WINDOW - SHIFT
        self.last = cols - self.west
        self.bands, self.across = rows // WINDOW, cols // WINDOW
        self.windows = self.bands * self.across
        self.local_windows = self.windows - self.bands
        self.window_rows, self.local_rows = self.windows * SLOT, self.local_windows * SLOT
        self.stride = up(cols, 16)
        self.own_rows = rows * self.stride
        self.west_rows = up(rows * self.west, 8)
        self.quad_lines, self.quad_cols, self.quad_west = rows // 2, cols // 2, self.west // 2
        self.quad_stride = up(self.quad_cols, 8)
        self.quad_count = up(self.quad_lines * self.quad_stride, 16)
        self.cot_stride = up(self.quad_cols, 16)
        self.cot_own = self.quad_lines * self.cot_stride
        self.cot_halo = up(self.quad_west * self.quad_lines, 16)

    def source(self, row, col):
        return row * self.stride + col if col >= 0 else self.own_rows + row * self.west + col + self.west

    def window_row(self, row, col):
        line = (row - SHIFT) % self.rows
        across, place = divmod(col + self.west, WINDOW)
        window = (across - 1) % self.across * self.bands + line // WINDOW
        return window * SLOT + line % WINDOW * (WINDOW + 1) + place

    def quad_row(self, row, col):
        phase = 2 * (col % 2) + row % 2
        return phase * self.quad_count + row // 2 * self.quad_stride + (col + self.west) // 2

    def onehot(self, shape, pairs):
        out = np.zeros(shape, np.float32)
        for i, j in pairs:
            out[i, j] = 1
        return jnp.asarray(out, jnp.bfloat16)

    def cells(self, first, last):
        return [(r, c) for r in range(self.rows) for c in range(first, last)]

    def to_windows(self):
        pairs = [(self.window_row(r, c), self.source(r, c)) for r, c in self.cells(-self.west, self.last)]
        return self.onehot((self.window_rows, self.own_rows + self.west_rows), pairs)

    def to_quads(self):
        pairs = [(self.quad_row(r, c), self.window_row(r, c)) for r, c in self.cells(-self.west, self.last)]
        return self.onehot((4 * self.quad_count, self.window_rows), pairs)

    def from_quads(self):
        return self.to_quads().T

    def pack_tokens(self):
        pairs = [
            (r * self.west + c - self.last, self.source(r, c)) for r, c in self.cells(self.last, self.cols)
        ]
        return self.onehot((self.west_rows, self.own_rows), pairs)

    def quad_cells(self, first, last):
        return [(i, j) for i in range(self.quad_lines) for j in range(first, last)]

    def pack_cot(self):
        first = self.quad_cols - self.quad_west
        pairs = [
            (self.quad_west * i + j - first, i * self.cot_stride + j)
            for i, j in self.quad_cells(first, self.quad_cols)
        ]
        return self.onehot((self.cot_halo, self.cot_own), pairs)

    def cot_to_quads(self):
        pairs = [
            (i * self.quad_stride + j, self.cot_own + self.quad_west * i + j)
            for i, j in self.quad_cells(0, self.quad_west)
        ]
        pairs += [
            (i * self.quad_stride + j, i * self.cot_stride + j - self.quad_west)
            for i, j in self.quad_cells(self.quad_west, self.quad_cols)
        ]
        return self.onehot((self.quad_count, self.cot_own + self.cot_halo), pairs)

    def tokens_back(self):
        pairs = [(r * self.west + c + self.west, self.window_row(r, c)) for r, c in self.cells(-self.west, 0)]
        return self.onehot((self.west_rows, self.window_rows), pairs)

    def quads_back(self):
        pairs = [
            (self.quad_west * i + j, i * self.quad_stride + j) for i, j in self.quad_cells(0, self.quad_west)
        ]
        return self.onehot((self.cot_halo, self.quad_count), pairs)

    def final_tokens(self):
        pairs = [(self.source(r, c), self.window_row(r, c)) for r, c in self.cells(0, self.last)]
        pairs += [
            (self.source(r, c), self.window_rows + r * self.west + c - self.last)
            for r, c in self.cells(self.last, self.cols)
        ]
        return self.onehot((self.own_rows, self.window_rows + self.west_rows), pairs)

    def final_quads(self):
        first = self.quad_cols - self.quad_west
        pairs = [
            (i * self.quad_stride + j, i * self.quad_stride + j + self.quad_west)
            for i, j in self.quad_cells(0, first)
        ]
        pairs += [
            (i * self.quad_stride + j, self.quad_count + self.quad_west * i + j - first)
            for i, j in self.quad_cells(first, self.quad_cols)
        ]
        return self.onehot((self.quad_count, self.quad_count + self.cot_halo), pairs)


def normalize(values):
    centred = values - jnp.mean(values, -1, keepdims=True)
    inverse_std = lax.rsqrt(jnp.mean(centred * centred, -1, keepdims=True) + EPS)
    return centred * inverse_std, inverse_std


def spread(ref, grid_ref, stride):
    ref[0 : grid_ref.shape[0] * stride, :] = jnp.zeros((grid_ref.shape[0] * stride, ref.shape[1]), ref.dtype)
    for line in range(grid_ref.shape[0]):
        ref[line * stride : line * stride + grid_ref.shape[1], :] = grid_ref[line]


def pack(grid, out, tokens, quads):
    out[0 : grid.west_rows, :] = tokens
    for part in range(quads.shape[1] // grid.channels):
        first = grid.west_rows + part * grid.cot_halo
        out[first : first + grid.cot_halo, :] = quads[:, part * grid.channels : (part + 1) * grid.channels]


def unpack(grid, ref, width):
    first = grid.west_rows
    parts = [
        ref[first + part * grid.cot_halo : first + (part + 1) * grid.cot_halo, :]
        for part in range(width // grid.channels)
    ]
    return ref[0 : grid.west_rows, :], jnp.concatenate(parts, 1)


def pre_kernel(grid, x, cot, pack_tokens, pack_cot, to_next, tokens, quads):
    spread(tokens, x.get(), grid.stride)
    spread(quads, cot.get(), grid.cot_stride)
    halo = pick(pack_cot.get()[...], quads[...])
    pack(grid, to_next.ref, pick(pack_tokens.get()[...], tokens[...]), halo)
    to_next.send()


def build_bias(grid, table, bias, mask):
    span, count = 2 * WINDOW - 1, WINDOW + 1
    per_group = LANES * grid.heads // grid.channels
    center = (WINDOW - 1) * span + WINDOW - 1
    rows = table.shape[1]
    values = jnp.concatenate([table[...], jnp.zeros((table.shape[0], 2 * LANES - rows), jnp.float32)], 1)
    key = lax.broadcasted_iota(jnp.int32, (SLOT, per_group * SLOT), 0)
    query = lax.broadcasted_iota(jnp.int32, (SLOT, per_group * SLOT), 1) & (SLOT - 1)
    key_row, key_col = key >> 3, key & (count - 1)
    query_row = query >> 3
    padded = jnp.where((key_row < WINDOW) & (key_col < WINDOW), 0.0, -1e30)
    key_late = (key_row >= WINDOW - SHIFT).astype(jnp.int32)
    query_late = (query_row >= WINDOW - SHIFT).astype(jnp.int32)
    mask[...] = jnp.where(key_late != query_late, -100.0, 0.0)
    place = lax.broadcasted_iota(jnp.int32, (LANES, per_group * SLOT), 0)
    lane = lax.broadcasted_iota(jnp.int32, (LANES, per_group * SLOT), 1)
    inside = lane & (SLOT - 1)
    wanted = (inside >> 3) * span + (inside & (count - 1))
    hit = (place == wanted) & ((inside >> 3) < WINDOW) & ((inside & (count - 1)) < WINDOW)
    for group in range(grid.heads // per_group):
        total = padded
        for head in range(per_group):
            line = jnp.broadcast_to(values[group * per_group + head : group * per_group + head + 1], (count, 2 * LANES))
            line = pltpu.roll(line, 0, 1, stride=1, stride_axis=0)
            blocks = [
                pltpu.roll(line, (span * r - center) % (2 * LANES), 1)[:, :LANES] for r in range(WINDOW)
            ]
            blocks.append(jnp.zeros((count, LANES), jnp.float32))
            block = jnp.concatenate(blocks, 0)
            high = block.astype(jnp.bfloat16)
            low = (block - high.astype(jnp.float32)).astype(jnp.bfloat16)
            select = jnp.where(hit & ((lane // SLOT) == head), 1.0, 0.0).astype(jnp.bfloat16)
            total = total + dot(high, select) + dot(low, select)
        bias[group] = total


class Heads:
    def __init__(self, grid, head_mask):
        self.channels = grid.channels
        self.head_size = grid.channels // grid.heads
        self.scale = self.head_size ** (-0.5)
        self.per_group = LANES // self.head_size
        self.groups = grid.heads // self.per_group
        self.head_mask = head_mask

    def spread(self, values):
        return jnp.concatenate([values] * self.per_group, 0) * self.head_mask

    def collect(self, stacked):
        total = None
        for head in range(self.per_group):
            part = stacked[head * SLOT : (head + 1) * SLOT, :]
            part = jnp.where(self.head_mask[head * SLOT : (head + 1) * SLOT, :] > 0, part, 0.0)
            total = part if total is None else total + part
        return total

    def split(self, projected, window, group):
        rows = slice(window * SLOT, (window + 1) * SLOT)
        firsts = [part * self.channels + group * LANES for part in range(3)]
        return [projected[rows, first : first + LANES] for first in firsts]

    def forward(self, jobs, fillers=()):
        def product(job):
            query, key, value = self.split(job.projected, job.window, job.group)
            return dot_t(key, self.spread(query)), value

        def soften(job, scores, value):
            scores = scores * self.scale + job.bias[job.group]
            if job.extra is not None:
                scores = scores + job.extra[...]
            weights = jnp.exp(scores - jnp.max(scores, 0, keepdims=True))
            prob = weights / jnp.sum(weights, 0, keepdims=True)
            job.probs[job.window * self.groups + job.group] = prob
            return prob.astype(jnp.bfloat16), value

        def mix(job, prob, value):
            return (dot(prob.T, value),)

        def store(job, mixed):
            rows, lanes = job.window * SLOT, job.group * LANES
            job.attended[rows : rows + SLOT, lanes : lanes + LANES] = self.collect(mixed).astype(jnp.bfloat16)
            return ()

        interleave(jobs, (product, soften, mix, store), fillers)

    def backward(self, jobs, outer, projected_grad, fillers=()):
        def rows_of(job):
            return slice(job.first + job.window * SLOT, job.first + (job.window + 1) * SLOT)

        def put(job, part, grad):
            at = part * self.channels + job.group * LANES
            projected_grad[rows_of(job), at : at + LANES] = grad.astype(jnp.bfloat16)

        def product(job):
            value = self.split(job.projected, job.window, job.group)[2]
            grads = self.spread(outer[rows_of(job), job.group * LANES : (job.group + 1) * LANES])
            prob = job.probs[job.window * self.groups + job.group]
            put(job, 2, dot(prob.astype(jnp.bfloat16), grads))
            return (dot_t(value, grads),)

        def soften(job, score_grad):
            prob = job.probs[job.window * self.groups + job.group]
            inner = jnp.sum(prob * score_grad, 0, keepdims=True)
            return ((prob * (score_grad - inner) * self.scale).astype(jnp.bfloat16),)

        def mix(job, soft):
            query, key, _ = self.split(job.projected, job.window, job.group)
            put(job, 1, dot(soft, self.spread(query)))
            return (dot(soft.T, key),)

        def store(job, mixed):
            put(job, 0, self.collect(mixed))
            return ()

        interleave(jobs, (product, soften, mix, store), fillers)


class Job:
    def __init__(self, **fields):
        self.__dict__.update(fields)


def jobs_of(windows, groups, **fields):
    return [Job(window=window, group=group, **fields) for window in range(windows) for group in range(groups)]


def interleave(jobs, stages, fillers=()):
    states = [()] * len(jobs)
    fillers = list(fillers)
    for turn in range(len(jobs) + len(stages) - 1):
        for depth, stage in enumerate(stages):
            at = turn - depth
            if 0 <= at < len(jobs):
                states[at] = stage(jobs[at], *states[at])
        if fillers:
            fillers.pop(0)()
    for filler in fillers:
        filler()


def with_masks(jobs, grid, mask):
    for job in jobs:
        job.extra = mask if job.window % grid.bands == grid.bands - 1 else None
    return jobs


def local_kernel(grid, x, cot, table, to_windows, attend_weight, head_mask, *rest):
    tokens = rest[-1]
    bias, mask, quads, windowed, normed, std, projected, attended, probs, orders, rolled_t, attended_t = [
        r.ref for r in rest[-13:-1]
    ]
    spread(quads, cot.get(), grid.cot_stride)
    spread(tokens, x.get(), grid.stride)
    build_bias(grid, table.get(), bias, mask)
    values = dot(to_windows.get()[:, : grid.own_rows], tokens[...])
    windowed[...] = values
    local = grid.local_rows
    n, inverse_std = normalize(values[:local])
    normed[...] = n
    std[...] = inverse_std
    projected[...] = dot(n.astype(jnp.bfloat16), attend_weight.get()[...]).astype(jnp.bfloat16)
    heads = Heads(grid, head_mask.get()[...])
    jobs = jobs_of(
        grid.local_windows, heads.groups, projected=projected, bias=bias, attended=attended, probs=probs
    )
    heads.forward(with_masks(jobs, grid, mask))
    rolled = n.astype(jnp.bfloat16)
    order = row_order(grid.channels)
    orders[...] = order
    rolled_t[...] = dot_t(order, rolled).astype(jnp.bfloat16)
    attended_t[...] = dot_t(order, attended[...]).astype(jnp.bfloat16)


def main_kernel(
    grid, from_west, to_windows, attend_weight, head_mask, bias, mask, to_quads, output_weight,
    cot_to_quads, merge_weight, from_quads, quads, windowed_own, normed_local, std_local, projected_local,
    attended_local, probs_local, orders, rolled_t_local, attended_t_local,
    kept, sent, projected_grad_out, normed_out, std_out, branch_grad_out, quad16_out,
    projected, attended, probs, outer, quad_grads, rolled_t, attended_t,
):
    channels, local = grid.channels, grid.local_rows
    west_tokens, west_quads = unpack(grid, from_west.get(), quads.ref.shape[1])
    windowed = windowed_own.ref[...] + dot(to_windows.ref[:, grid.own_rows :], west_tokens)
    normed, inverse_std = normalize(windowed[local:])
    normed_out.ref[:local] = normed_local.ref[...]
    normed_out.ref[local:] = normed
    std_out.ref[:local] = std_local.ref[...]
    std_out.ref[local:] = inverse_std
    projected[...] = dot(normed.astype(jnp.bfloat16), attend_weight.ref[...]).astype(jnp.bfloat16)
    rolled = normed.astype(jnp.bfloat16)
    cot_select = cot_to_quads.ref
    cot_quads = dot(cot_select[:, : grid.cot_own], quads.ref[: grid.cot_own, :])
    cot_quads = (cot_quads + dot(cot_select[:, grid.cot_own :], west_quads)).astype(jnp.bfloat16)
    merge_ref = merge_weight.ref

    def quad_product(k):
        quad_grads[k] = dot_t(cot_quads, merge_ref[k * channels : (k + 1) * channels, :])

    heads = Heads(grid, head_mask.ref[...])
    jobs = jobs_of(grid.bands, heads.groups, projected=projected, bias=bias.ref, attended=attended, probs=probs)
    heads.forward(
        with_masks(jobs, grid, mask.ref), [functools.partial(quad_product, k) for k in range(4)]
    )

    select = to_quads.ref
    attended_quads = (
        dot(select[:, :local], attended_local.ref[...]) + dot(select[:, local:], attended[...])
    ).astype(jnp.bfloat16)
    feature_quads = dot(select[...], windowed.astype(jnp.bfloat16))
    branch = dot(attended_quads, output_weight.ref[...])
    hidden = (feature_quads + branch).astype(jnp.bfloat16).astype(jnp.float32)
    count = grid.quad_count
    phases = [hidden[k * count : (k + 1) * count] for k in range(4)]
    width = 4 * channels
    mean = sum(jnp.sum(phase, -1, keepdims=True) for phase in phases) / width
    centred = [phase - mean for phase in phases]
    variance = sum(jnp.sum(phase * phase, -1, keepdims=True) for phase in centred) / width
    quad_std = lax.rsqrt(variance + EPS)
    quad_normed = [phase * quad_std for phase in centred]
    for k in range(4):
        quad16_out.ref[k * count : (k + 1) * count, :] = quad_normed[k].astype(jnp.bfloat16)
    first = sum(jnp.sum(quad_grads[k], -1, keepdims=True) for k in range(4)) / width
    second = sum(jnp.sum(quad_grads[k] * quad_normed[k], -1, keepdims=True) for k in range(4)) / width
    hidden_grad = jnp.concatenate(
        [quad_std * (quad_grads[k] - first - quad_normed[k] * second) for k in range(4)], 0
    ).astype(jnp.bfloat16)
    branch_grad = pick(from_quads.ref[...], hidden_grad)
    branch_grad_out.ref[...] = branch_grad
    outer[...] = dot_t(branch_grad, output_weight.ref[...]).astype(jnp.bfloat16)
    projected_grad = projected_grad_out.ref
    jobs = jobs_of(
        grid.local_windows, heads.groups, projected=projected_local.ref, probs=probs_local.ref, first=0
    )
    jobs += jobs_of(grid.bands, heads.groups, projected=projected, probs=probs, first=local)

    def turned():
        rolled_t[...] = dot_t(orders.ref[...], rolled).astype(jnp.bfloat16)

    def turned_attended():
        attended_t[...] = dot_t(orders.ref[...], attended[...]).astype(jnp.bfloat16)

    heads.backward(jobs, outer, projected_grad, [turned_attended, turned])

    half, joint = channels // 2, 3 * channels

    def put(first, local_t, halo_t, grads):
        piece = dot(local_t, grads[:local]) + dot(halo_t, grads[local:])
        kept.ref[:, first : first + piece.shape[1]] = piece[:half]
        sent.ref[:, first : first + piece.shape[1]] = piece[half:].astype(jnp.bfloat16)

    put(joint, attended_t_local.ref[...], attended_t[...], branch_grad)
    for first in range(0, joint, channels):
        put(first, rolled_t_local.ref[...], rolled_t[...], projected_grad[:, first : first + channels])


def tail_kernel(
    grid, projected_grad, attend_weight, normed, inverse_std, branch_grad, quads_back, tokens_back, merged,
    back, feature_grads,
):
    grads = dot_t(projected_grad.get()[...], attend_weight.get()[...])
    n = normed.get()[...]
    first = jnp.mean(grads, -1, keepdims=True)
    second = jnp.mean(grads * n, -1, keepdims=True)
    rolled_grad = inverse_std.get()[...] * (grads - first - n * second)
    total = (branch_grad.get()[...].astype(jnp.float32) + rolled_grad).astype(jnp.bfloat16)
    feature_grads.ref[...] = total
    feature_grads.send()
    pack(grid, back.ref, pick(tokens_back.get()[...], total), pick(quads_back.get()[...], merged.get()[...]))
    back.send()


def merge_kernel(grid, quad16, merge_weight, merged):
    channels, count = grid.channels, grid.quad_count
    sums = None
    quad_ref, merge_ref = quad16.get(), merge_weight.get()
    for k in range(4):
        term = dot(quad_ref[k * count : (k + 1) * count, :], merge_ref[k * channels : (k + 1) * channels, :])
        sums = term if sums is None else sums + term
    merged.ref[...] = sums.astype(jnp.bfloat16)
    merged.send()


def last_kernel(grid, feature_grads, merged, came, final_tokens, final_quads, out, merged_out):
    width = merged_out.ref.shape[2]
    tokens, quads = unpack(grid, came.get(), width)
    rows = grid.window_rows
    select = final_tokens.get()
    total = dot(select[:, :rows], feature_grads.get()[...]) + dot(select[:, rows:], tokens)
    for line in range(grid.rows):
        out.ref[line] = total[line * grid.stride : line * grid.stride + grid.cols].astype(jnp.bfloat16)
    out.send()
    select = final_quads.get()
    count = grid.quad_count
    sums = dot(select[:, :count], merged.get()[...]) + dot(select[:, count:], quads)
    for line in range(grid.quad_lines):
        first = line * grid.quad_stride
        merged_out.ref[line] = sums[first : first + grid.quad_cols].astype(jnp.bfloat16)
    merged_out.send()


class Operand:
    def __init__(self, source, ref, sem):
        self.ref, self.copy, self.waited = ref, pltpu.make_async_copy(source, ref, sem), False
        self.copy.start()

    def get(self):
        if not self.waited:
            self.copy.wait()
            self.waited = True
        return self.ref


class Result:
    def __init__(self, target, ref, sem):
        self.ref, self.copy = ref, pltpu.make_async_copy(ref, target, sem)

    def send(self):
        self.copy.start()

    def wait(self):
        self.copy.wait()


class Held:
    def __init__(self, array):
        self.array = array


class Load:
    def __init__(self, array):
        self.array = array


class HeldRef:
    def __init__(self, ref):
        self.ref = ref

    def get(self):
        return self.ref

    def send(self):
        pass

    def wait(self):
        pass


def call(kernel, outs, *args, scratch=()):
    given = [getattr(arg, "array", arg) for arg in args]
    loads = [arg.array for arg in args if isinstance(arg, Load)]
    made = [*[Held(load) for load in loads], *outs]
    plain = [arg for arg in args if not isinstance(arg, (Held, Load))]
    plain += [out for out in outs if not isinstance(out, Held)]

    def body(*refs):
        refs = list(refs)
        ins, refs = refs[: len(given)], refs[len(given) :]
        loaded, refs = refs[: len(loads)], refs[len(loads) :]
        results, refs = refs[: len(outs)], refs[len(outs) :]
        inner, refs = refs[: len(scratch)], refs[len(scratch) :]
        buffers, sems = refs[:-1], refs[-1]
        count = 0
        operands = []
        for arg, ref in zip(args, ins):
            if isinstance(arg, Held):
                operands.append(HeldRef(ref))
                continue
            target = loaded.pop(0) if isinstance(arg, Load) else buffers.pop(0)
            operands.append(Operand(ref, target, sems.at[count]))
            count += 1
        outputs = []
        for out, ref in zip(outs, results):
            if isinstance(out, Held):
                outputs.append(HeldRef(ref))
                continue
            outputs.append(Result(ref, buffers.pop(0), sems.at[count]))
            count += 1
        kernel(*operands, *outputs, *inner)
        for operand in operands:
            operand.get()
        for output in outputs:
            output.wait()

    def space(item):
        return pltpu.VMEM if isinstance(item, Held) else pltpu.HBM

    results = pl.pallas_call(
        body,
        out_shape=[space(m)(getattr(m, "array", m).shape, getattr(m, "array", m).dtype) for m in made],
        in_specs=[pl.BlockSpec(memory_space=space(arg)) for arg in args],
        out_specs=[pl.BlockSpec(memory_space=space(m)) for m in made],
        scratch_shapes=[
            *scratch,
            *[pltpu.VMEM(a.shape, a.dtype) for a in plain],
            pltpu.SemaphoreType.DMA((max(len(plain) + len(loads), 1),)),
        ],
        compiler_params=pltpu.CompilerParams(vmem_limit_bytes=24 * 2**20),
    )(*[pltpu.with_memory_space_constraint(a, space(arg)) for a, arg in zip(given, args)])
    return [Held(result) if isinstance(m, Held) else result for result, m in zip(results, made)]


def f32(*shape):
    return jax.ShapeDtypeStruct(shape, jnp.float32)


def b16(*shape):
    return jax.ShapeDtypeStruct(shape, jnp.bfloat16)


def held(shape):
    return Held(shape)


def bit_groups():
    frame_bits = lax.axis_size("frame").bit_length() - 1
    azim_bits = lax.axis_size("azim").bit_length() - 1
    frame = [1 << bit for bit in range(frame_bits)]
    azim = [1 << (bit + frame_bits) for bit in range(azim_bits)]
    return [frame[:1], azim[:1] + frame[1:2], azim[:0:-1] + frame[:1:-1]]


def exchange(block, mask):
    members = lax.axis_size(("azim", "frame"))
    return lax.ppermute(block, ("azim", "frame"), [(i, i ^ mask) for i in range(members)])


def row_order(channels):
    row = lax.broadcasted_iota(jnp.int32, (channels, channels), 0)
    column = lax.broadcasted_iota(jnp.int32, (channels, channels), 1)
    weights = sum(bit_groups(), [])
    members = 1 << len(weights)
    if channels % members == 0:
        each = channels // members
        me = lax.axis_index("azim") * lax.axis_size("frame") + lax.axis_index("frame")
        part = jnp.floor((row.astype(jnp.float32) + 0.5) * (1.0 / each)).astype(jnp.int32)
        row = row - part * each
        for stage, weight in enumerate(weights):
            far = (part >> (len(weights) - 1 - stage)) & 1
            own = (me >> (weight.bit_length() - 1)) & 1
            row = row + (far ^ own) * (weight * each)
    return jnp.where(column == row, 1.0, 0.0).astype(jnp.bfloat16)


def scatter_flat(terms):
    weights = sum(bit_groups(), [])
    members = 1 << len(weights)
    widths = [term.size // members for term in terms]
    held = jnp.concatenate([term.reshape(members, -1) for term in terms], 1).astype(jnp.bfloat16)
    held = held.reshape((2,) * len(weights) + (-1,))
    me = lax.axis_index(("azim", "frame"))
    for weight in weights:
        dim = len(weights) - weight.bit_length()
        own = (me >> (weight.bit_length() - 1)) & 1
        kept = lax.dynamic_slice_in_dim(held, own, 1, dim)
        got = exchange(lax.dynamic_slice_in_dim(held, 1 - own, 1, dim), weight)
        total = kept.astype(jnp.float32) + got.astype(jnp.float32)
        held = total.astype(jnp.bfloat16)
    total = total.reshape(-1)
    return total[: widths[0]], total[widths[0] :]


def send_block(part, weights, block):
    mask = sum(w for i, w in enumerate(weights) if block >> (len(weights) - 1 - i) & 1)
    return exchange(part.astype(jnp.bfloat16), mask)


def add_kernel(first, kept, got, *totals):
    at = 0
    for total in totals:
        rows = total.ref.shape[0]
        own = kept.ref[first + at : first + at + rows, :]
        total.ref[...] = (own + got.ref[at : at + rows, :].astype(jnp.float32)).astype(total.ref.dtype)
        at += rows


def finish_kernel(split, total, *rest):
    gots, (attend_grad, output_grad) = rest[:-2], rest[-2:]
    rows = gots[0].ref.shape[0]
    sums = total.get()[:rows, :]
    for got in gots:
        sums = sums + got.get()[...].astype(jnp.float32)
    for out, first, last in ((attend_grad, 0, split), (output_grad, split, sums.shape[1])):
        tiles = (last - first) // LANES
        for tile in range(tiles):
            at = first + tile * LANES
            out.ref[pl.ds(tile, rows, stride=tiles), :] = sums[:, at : at + LANES]
        out.send()


def scatter_sum(kept, sent, channels):
    groups = bit_groups()
    split = 3 * channels
    if channels % (1 << len(sum(groups, []))):
        whole = jnp.concatenate([kept, sent.astype(jnp.float32)], 0)
        return scatter_flat((whole[:, :split], whole[:, split:]))
    count = 1 << len(groups[1])
    rows, width = kept.shape[0] // count, kept.shape[1]
    pieces = {}
    for first, last in ((count // 2, count), (0, count // 2)):
        got = exchange(sent[first * rows : last * rows], groups[0][0])
        shapes = [held(b16(rows, width) if block else f32(rows, width)) for block in range(first, last)]
        sums = call(functools.partial(add_kernel, first * rows), shapes, Held(kept), Held(got))
        pieces.update({block: total.array for block, total in zip(range(first, last), sums)})
    gots = [send_block(pieces[block], groups[1], block) for block in range(count - 1, 0, -1)]
    total = sum((got.astype(jnp.float32) for got in gots), pieces[0])
    rows = total.shape[0] >> len(groups[2])
    blocks = sorted(range(1, 1 << len(groups[2])), key=lambda block: (block != 2, block))
    gots = [send_block(total[block * rows : (block + 1) * rows], groups[2], block) for block in blocks]
    attend_grad, output_grad = call(
        functools.partial(finish_kernel, split),
        (f32(rows * split // LANES, LANES), f32(rows * channels // LANES, LANES)),
        Held(total), *[Held(got) for got in gots],
    )
    return attend_grad.reshape(-1), output_grad.reshape(-1)


def from_behind(block, axis, distance):
    size = lax.axis_size(axis)
    return lax.ppermute(block, axis, [((i - distance) % size, i) for i in range(size)])


def per_device(features, position_bias, attend_weight, output_weight, merge_weight, cotangent):
    x, cot = features[0], cotangent[0]
    rows, cols, channels = x.shape
    heads = position_bias.shape[1]
    grid = Grid(rows, cols, heads, channels)
    width = cot.shape[2]
    bf16 = jnp.bfloat16
    halo_rows = grid.west_rows + width // channels * grid.cot_halo
    own, local, quads = grid.window_rows, grid.local_rows, 4 * grid.quad_count
    per_group = LANES * heads // channels
    groups, across = heads // per_group, per_group * SLOT
    lane_head = np.arange(LANES) // (channels // heads)
    head_mask = jnp.asarray(np.repeat(np.arange(per_group), SLOT)[:, None] == lane_head[None, :]).astype(bf16)
    (to_next,) = call(
        functools.partial(pre_kernel, grid), (held(b16(halo_rows, channels)),),
        x, cot, grid.pack_tokens(), grid.pack_cot(),
        scratch=[pltpu.VMEM((grid.own_rows, channels), bf16), pltpu.VMEM((grid.cot_own, width), bf16)],
    )
    from_west = Held(from_behind(to_next.array, "azim", 1))
    halo = grid.bands * SLOT
    (
        to_windows, attend_held, mask_held, merge_held, output_held, to_quads, cot_to_quads, from_quads, quads_back,
        tokens_back, final_tokens, final_quads, bias, mask, quad_tokens, windowed, normed_local, std_local,
        projected, attended, probs, orders, rolled_t, attended_t,
    ) = call(
        functools.partial(local_kernel, grid),
        (
            held(f32(groups, SLOT, across)), held(f32(SLOT, across)), held(b16(grid.cot_own, width)),
            held(f32(own, channels)), held(f32(local, channels)), held(f32(local, 1)),
            held(b16(local, 3 * channels)), held(b16(local, channels)),
            held(f32(grid.local_windows * groups, SLOT, across)),
            held(b16(channels, channels)),
            held(b16(channels, local)), held(b16(channels, local)),
        ),
        x, cot, position_bias.T, Load(grid.to_windows()), Load(attend_weight), Load(head_mask), Load(merge_weight),
        Load(output_weight), Load(grid.to_quads()), Load(grid.cot_to_quads()), Load(grid.from_quads()),
        Load(grid.quads_back()), Load(grid.tokens_back()), Load(grid.final_tokens()), Load(grid.final_quads()),
        scratch=[pltpu.VMEM((grid.own_rows, channels), bf16)],
    )
    half = channels // 2
    kept, sent, projected_grad, normed, inverse_std, branch_grad, quad16 = call(
        functools.partial(main_kernel, grid),
        (
            held(f32(half, 4 * channels)), held(b16(half, 4 * channels)), held(b16(own, 3 * channels)),
            held(f32(own, channels)), held(f32(own, 1)), held(b16(own, channels)), held(b16(quads, channels)),
        ),
        from_west, to_windows, attend_held, mask_held, bias, mask, to_quads, output_held, cot_to_quads, merge_held,
        from_quads, quad_tokens, windowed, normed_local, std_local, projected, attended, probs, orders,
        rolled_t, attended_t,
        scratch=[
            pltpu.VMEM((halo, 3 * channels), bf16),
            pltpu.VMEM((halo, channels), bf16),
            pltpu.VMEM((grid.bands * groups, SLOT, across), jnp.float32),
            pltpu.VMEM((own, channels), bf16),
            pltpu.VMEM((4, grid.quad_count, channels), jnp.float32),
            pltpu.VMEM((channels, halo), bf16),
            pltpu.VMEM((channels, halo), bf16),
        ],
    )
    (merged_quads,) = call(
        functools.partial(merge_kernel, grid), (held(b16(grid.quad_count, width)),), quad16, merge_held
    )
    back, feature_grads = call(
        functools.partial(tail_kernel, grid), (held(b16(halo_rows, channels)), held(b16(own, channels))),
        projected_grad, attend_held, normed, inverse_std, branch_grad, quads_back, tokens_back, merged_quads,
    )
    came = Held(from_behind(back.array, "azim", -1))
    feature_grad, merged = call(
        functools.partial(last_kernel, grid),
        (b16(rows, cols, channels), b16(grid.quad_lines, grid.quad_cols, width)),
        feature_grads, merged_quads, came, final_tokens, final_quads,
    )
    attend_grad, output_grad = scatter_sum(kept.array, sent.array, channels)
    return (merged[None], feature_grad[None], attend_grad, output_grad)


def solution(mesh):
    in_specs = (P("frame", None, "azim", None), P(), P(), P(), P(), P("frame", None, "azim", None))
    out_specs = (
        P("frame", None, "azim", None),
        P("frame", None, "azim", None),
        P(("azim", "frame")),
        P(("azim", "frame")),
    )

    return jax.shard_map(per_device, mesh=mesh, in_specs=in_specs, out_specs=out_specs, check_vma=False)
```
